32 devices in a mesh: gx: 4 (over z), gy: 4 (over y, core), gz: 2 (over x).
Axes of the slice: x: 2, y: 2, z: 4, core: 2. Of those that a mesh axis runs over, the one named last changes fastest.
Arguments:
- node_irreps: bfloat16 [4, 4, 2, 16, 25, 128], P('gx', 'gy', 'gz'), may hold values from -5 to 11
- positions: float32 [4, 4, 2, 3, 16], P('gx', 'gy', 'gz'), may hold values from 0 to 6.8
- send_list: int32 [4, 4, 2, 8], P('gx', 'gy', 'gz'), may hold values from 0 to 15, as said below
- neighbours: int32 [4, 4, 2, 16, 32], P('gx', 'gy', 'gz'), may hold values from 0 to 231
- displacements: float32 [4, 4, 2, 3, 512], P('gx', 'gy', 'gz'), may hold values from -6 to 6
- order_zero: bfloat16 [640, 640], replicated, may hold values from -0.25 to 0.25
- order_one: bfloat16 [512, 1024], replicated, may hold values from -0.25 to 0.25
- order_two: bfloat16 [384, 768], replicated, may hold values from -0.3125 to 0.3125
- reciprocal_triples: int32 [1024, 3], replicated, may hold values from -6 to 6
- reciprocal_filter: float32 [1024, 128], replicated, may hold values from 0.1 to 1
- cotangent: float32 [4, 4, 2, 16, 128], P('gx', 'gy', 'gz'), may hold values from -5 to 11
Outputs:
- updated: bfloat16 [4, 4, 2, 16, 25, 128], P('gx', 'gy', 'gz')
- long_range: float32 [4, 4, 2, 16, 128], P('gx', 'gy', 'gz')
- charge_grad: float32 [4, 4, 2, 16, 128], P('gx', 'gy', 'gz')
- position_grad: float32 [4, 4, 2, 3, 16], P('gx', 'gy', 'gz')
The draws below stay inside these ranges and needn't reach their ends.
Inputs may be any that keep to these rules, and one draw needn't show every extreme that they name: `send_list`: entries of one block are distinct atoms of that block.
All inputs are finite; a program needn't handle non-finite values.
Results may differ from the reference program's by a relative error of at most 0.0023.
Values may be sent and summed in bfloat16 or wider, within the bound.
No kernel may reach another device: no remote copies, remote signals or barrier semaphores. Data moves between devices by JAX's collectives and lax.ppermute only.
A program may use at most 64 MiB of HBM per device.

```python
import math
import jax
import jax.numpy as jnp
from jax import lax

CHANNEL_COUNT = 128
HARMONICS = 25
NEIGHBOURS = 32
WAVE_VECTORS = 1024
ATOMS_DEV = 16
GHOSTS = 8
BLOCKS_X = 4
BLOCKS_Y = 4
BLOCKS_Z = 2


def rising_field(key, trailing):
    noise_key, scale_key = jax.random.split(key, 2)
    shape = (BLOCKS_X, BLOCKS_Y, BLOCKS_Z, ATOMS_DEV) + trailing
    noise = jax.random.truncated_normal(noise_key, -5.0, 5.0, shape, jnp.float32)
    channel_scale = jnp.exp(jax.random.uniform(scale_key, (CHANNEL_COUNT,), jnp.float32, math.log(0.5), math.log(2.0)))
    rising = 1.0 + 2.0 * jnp.arange(BLOCKS_X, dtype=jnp.float32) / max(BLOCKS_X - 1, 1)
    offset = rising[:, None, None, None, None] * channel_scale
    return (noise, offset)


def draw_node_irreps(key, part):
    noise, offset = rising_field(jax.random.fold_in(key, 11), (HARMONICS, CHANNEL_COUNT))
    return noise.at[:, :, :, :, 0, :].add(offset).astype(jnp.bfloat16)


def draw_cotangent(key, part):
    noise, offset = rising_field(jax.random.fold_in(key, 23), (CHANNEL_COUNT,))
    return (noise + offset).astype(jnp.float32)


def draw_send_list(key, part):
    blocks_total = BLOCKS_X * BLOCKS_Y * BLOCKS_Z
    block_keys = jax.random.split(jax.random.fold_in(key, 37), blocks_total)
    chosen = jax.vmap(lambda one_key: jax.random.permutation(one_key, ATOMS_DEV)[:GHOSTS])(block_keys)
    return chosen.reshape(BLOCKS_X, BLOCKS_Y, BLOCKS_Z, GHOSTS).astype(jnp.int32)


def touch_ends(values, stream_key, low, top_value):
    longest = values.shape.index(max(values.shape))
    spots = []
    for shift in (0, 1):
        where = [jax.random.randint(jax.random.fold_in(stream_key, axis), (), 0, length) for axis, length in enumerate(values.shape)]
        where[longest] = (where[longest] + shift) % values.shape[longest]
        spots.append(tuple(where))
    return values.at[spots[0]].set(low).at[spots[1]].set(top_value)


def steps_of(own_key, dims, shards, smallest, top_value):
    def one(position, parts):
        draws = jax.random.uniform(jax.random.fold_in(jax.random.fold_in(own_key, 6), position), (parts,), jnp.float32, smallest / len(shards), top_value / len(shards))
        return jnp.repeat(jnp.exp(draws), dims[position] // parts).reshape((-1,) + (1,) * (len(dims) - position - 1))

    loudness = one(*shards[0])
    for cut in shards[1:]:
        loudness = loudness * one(*cut)
    return loudness


def centred(own_key, extent, deviation, most, kind=jnp.bfloat16):
    values = deviation * jax.random.normal(own_key, extent, jnp.float32)
    return jnp.clip(values, min=-most, max=most).astype(kind)


def setup_inputs(seed: int = 0) -> dict:
    seeds = jax.random.split(jax.random.key(seed), 12)
    return {
        "node_irreps": draw_node_irreps(jax.random.fold_in(seeds[11], 71), 0),
        "positions": jnp.clip(6.8 * jax.random.uniform(seeds[1], (BLOCKS_X, BLOCKS_Y, BLOCKS_Z, 3, ATOMS_DEV), jnp.float32) ** steps_of(seeds[1], (BLOCKS_X, BLOCKS_Y, BLOCKS_Z, 3, ATOMS_DEV), ((0, 4), (1, 4), (2, 2)), -0.2, 0.2), 0.0, 6.8),
        "send_list": draw_send_list(jax.random.fold_in(seeds[11], 71), 0),
        "neighbours": touch_ends(jax.random.randint(seeds[3], (BLOCKS_X, BLOCKS_Y, BLOCKS_Z, ATOMS_DEV, NEIGHBOURS), 0, ATOMS_DEV + 27 * GHOSTS), jax.random.fold_in(seeds[3], 1), 0, (ATOMS_DEV + 27 * GHOSTS) - 1).astype(jnp.int32),
        "displacements": jnp.clip(jax.random.uniform(seeds[4], (BLOCKS_X, BLOCKS_Y, BLOCKS_Z, 3, ATOMS_DEV * NEIGHBOURS), jnp.float32, -6.0, 6.0) * steps_of(seeds[4], (BLOCKS_X, BLOCKS_Y, BLOCKS_Z, 3, ATOMS_DEV * NEIGHBOURS), ((0, 4), (1, 4), (2, 2)), -0.4, 0.0), -6.0, 6.0),
        "order_zero": centred(seeds[5], (5 * CHANNEL_COUNT, 5 * CHANNEL_COUNT), (5 * CHANNEL_COUNT) ** -0.5, 0.25),
        "order_one": centred(seeds[6], (4 * CHANNEL_COUNT, 8 * CHANNEL_COUNT), (4 * CHANNEL_COUNT) ** -0.5, 0.25),
        "order_two": centred(seeds[7], (3 * CHANNEL_COUNT, 6 * CHANNEL_COUNT), (3 * CHANNEL_COUNT) ** -0.5, 0.3125),
        "reciprocal_triples": touch_ends(jax.random.randint(seeds[8], (WAVE_VECTORS, 3), -6, 7), jax.random.fold_in(seeds[8], 1), -6, 6).astype(jnp.int32),
        "reciprocal_filter": jnp.clip(jnp.exp(jax.random.uniform(seeds[9], (WAVE_VECTORS, CHANNEL_COUNT), jnp.float32, math.log(0.1), math.log(1.0))), 0.1, 1.0),
        "cotangent": draw_cotangent(jax.random.fold_in(seeds[11], 71), 0),
    }


highest = lax.Precision.HIGHEST
cell_length = 6.8
planar_floor = 0.25
radial_width = 64.0

def harmonic_slot(degree, signed_order):
    return degree * degree + degree + signed_order

def kept_rows(keep_all):
    layout = []
    for degree in range(5):
        for signed_order in range(-degree, degree + 1):
            if keep_all or abs(signed_order) <= 2:
                layout.append(harmonic_slot(degree, signed_order))
    return layout

def edge_messages(lookup_table, displacement, neighbour_index, order_zero, order_one, order_two, layout):
    atom_count = neighbour_index.shape[0]
    neighbour_count = neighbour_index.shape[1]
    flat_index = neighbour_index.reshape(-1)
    edge_count = flat_index.shape[0]
    feature_width = lookup_table.shape[2]
    source = lookup_table[flat_index]
    length_squared = lax.optimization_barrier(jnp.sum(displacement * displacement, axis=0))
    radial = jnp.exp(-length_squared / radial_width) / math.sqrt(neighbour_count)
    planar = jnp.sqrt(displacement[0] * displacement[0] + displacement[1] * displacement[1] + planar_floor)
    cos_one = displacement[0] / planar
    sin_one = displacement[1] / planar

    def neighbour_sum(values):
        weighted = values * radial[:, None, None]
        return lax.optimization_barrier(jnp.sum(weighted.reshape(atom_count, neighbour_count, values.shape[1], feature_width), axis=1))
    collected = {}
    zero_slots = [layout.index(harmonic_slot(degree, 0)) for degree in range(5)]
    zero_input = source[:, zero_slots, :].reshape(edge_count, 5 * feature_width)
    zero_output = jnp.dot(zero_input, order_zero, preferred_element_type=jnp.float32)
    summed_zero_part = neighbour_sum(zero_output.reshape(edge_count, 5, feature_width))
    for degree in range(5):
        collected[harmonic_slot(degree, 0)] = summed_zero_part[:, degree]
    rotations = ((1, cos_one, sin_one, order_one), (2, cos_one * cos_one - sin_one * sin_one, 2.0 * cos_one * sin_one, order_two))
    for harmonic_order, cosine, sine_term, weight_pair in rotations:
        degrees = list(range(harmonic_order, 5))
        count_of_rows = len(degrees)
        plus_slots = [layout.index(harmonic_slot(degree, harmonic_order)) for degree in degrees]
        minus_slots = [layout.index(harmonic_slot(degree, -harmonic_order)) for degree in degrees]
        plus_part = source[:, plus_slots, :].astype(jnp.float32)
        minus_part = source[:, minus_slots, :].astype(jnp.float32)
        cosine_wide = cosine[:, None, None]
        sine_wide = sine_term[:, None, None]
        turned_plus = (cosine_wide * plus_part + sine_wide * minus_part).astype(jnp.bfloat16)
        turned_minus = (cosine_wide * minus_part - sine_wide * plus_part).astype(jnp.bfloat16)
        split_at = count_of_rows * feature_width
        stacked = jnp.concatenate([turned_plus.reshape(edge_count, split_at), turned_minus.reshape(edge_count, split_at)], axis=0)
        product = jnp.dot(stacked, weight_pair, preferred_element_type=jnp.float32)
        upper_half = product[:edge_count]
        lower_half = product[edge_count:]
        mixed_plus = (upper_half[:, :split_at] - lower_half[:, split_at:]).reshape(edge_count, count_of_rows, feature_width)
        mixed_minus = (upper_half[:, split_at:] + lower_half[:, :split_at]).reshape(edge_count, count_of_rows, feature_width)
        back_plus = neighbour_sum(cosine_wide * mixed_plus - sine_wide * mixed_minus)
        back_minus = neighbour_sum(sine_wide * mixed_plus + cosine_wide * mixed_minus)
        for position_in, degree in enumerate(degrees):
            collected[harmonic_slot(degree, harmonic_order)] = back_plus[:, position_in]
            collected[harmonic_slot(degree, -harmonic_order)] = back_minus[:, position_in]
    zero_block = jnp.zeros((atom_count, feature_width), jnp.float32)
    return jnp.stack([collected.get(slot_number, zero_block) for slot_number in range(25)], axis=1)

def reference(node_irreps, positions, send_list, neighbours, displacements, order_zero, order_one, order_two, reciprocal_triples, reciprocal_filter, cotangent):
    blocks_total = BLOCKS_X * BLOCKS_Y * BLOCKS_Z
    irreps_flat = node_irreps.reshape(blocks_total, ATOMS_DEV, HARMONICS, CHANNEL_COUNT)
    sent_flat = jax.vmap(lambda block_rows, chosen: block_rows[chosen])(irreps_flat, send_list.reshape(blocks_total, GHOSTS))
    displacement_flat = displacements.reshape(blocks_total, 3, ATOMS_DEV * NEIGHBOURS)
    neighbour_flat = neighbours.reshape(blocks_total, ATOMS_DEV, NEIGHBOURS)
    layout = kept_rows(True)

    def one_block(flat_block):
        block_x = flat_block // (BLOCKS_Y * BLOCKS_Z)
        block_y = flat_block // BLOCKS_Z % BLOCKS_Y
        block_z = flat_block % BLOCKS_Z
        pieces = []
        for shift_x in range(3):
            for shift_y in range(3):
                for shift_z in range(3):
                    other_x = (block_x + shift_x - 1) % BLOCKS_X
                    other_y = (block_y + shift_y - 1) % BLOCKS_Y
                    other_z = (block_z + shift_z - 1) % BLOCKS_Z
                    other_block = (other_x * BLOCKS_Y + other_y) * BLOCKS_Z + other_z
                    pieces.append(sent_flat[other_block.astype(jnp.int32)])
        lookup_table = jnp.concatenate([irreps_flat[flat_block]] + pieces, axis=0)
        messages = edge_messages(lookup_table, displacement_flat[flat_block], neighbour_flat[flat_block], order_zero, order_one, order_two, layout)
        return (irreps_flat[flat_block].astype(jnp.float32) + messages).astype(jnp.bfloat16)
    updated = lax.map(one_block, jnp.arange(blocks_total, dtype=jnp.int32)).reshape(node_irreps.shape)
    total_atom_count = ATOMS_DEV * blocks_total
    scale_factor = 1.0 / math.sqrt(total_atom_count * WAVE_VECTORS)
    corner = jnp.stack(jnp.meshgrid(jnp.arange(BLOCKS_X), jnp.arange(BLOCKS_Y), jnp.arange(BLOCKS_Z), indexing='ij'), axis=-1).astype(jnp.float32)
    global_place = positions + cell_length * corner[:, :, :, :, None]
    box = cell_length * jnp.array([BLOCKS_X, BLOCKS_Y, BLOCKS_Z], jnp.float32)
    fractional = global_place / box[:, None]
    fractional = jnp.transpose(fractional, (0, 1, 2, 4, 3)).reshape(total_atom_count, 3)
    wave_float = reciprocal_triples.astype(jnp.float32)
    phase = 2.0 * math.pi * jnp.dot(fractional, wave_float.T, precision=highest)
    cos_table = jnp.cos(phase)
    sin_table = jnp.sin(phase)
    charges = node_irreps[:, :, :, :, 0, :].astype(jnp.float32).reshape(total_atom_count, CHANNEL_COUNT)
    centered = charges - lax.optimization_barrier(jnp.sum(charges, axis=0)) / total_atom_count
    struct_cos = jnp.dot(cos_table.T, centered, precision=highest)
    struct_sin = jnp.dot(sin_table.T, centered, precision=highest)
    long_range = scale_factor * (jnp.dot(cos_table, reciprocal_filter * struct_cos, precision=highest) + jnp.dot(sin_table, reciprocal_filter * struct_sin, precision=highest))
    grad_input = cotangent.reshape(total_atom_count, CHANNEL_COUNT)
    resp_cos = jnp.dot(cos_table.T, grad_input, precision=highest)
    resp_sin = jnp.dot(sin_table.T, grad_input, precision=highest)
    charge_term = scale_factor * (jnp.dot(cos_table, reciprocal_filter * resp_cos, precision=highest) + jnp.dot(sin_table, reciprocal_filter * resp_sin, precision=highest))
    charge_grad = charge_term - lax.optimization_barrier(jnp.sum(charge_term, axis=0)) / total_atom_count
    with_sin = jnp.dot(grad_input, (reciprocal_filter * struct_sin).T, precision=highest) + jnp.dot(centered, (reciprocal_filter * resp_sin).T, precision=highest)
    with_cos = jnp.dot(grad_input, (reciprocal_filter * struct_cos).T, precision=highest) + jnp.dot(centered, (reciprocal_filter * resp_cos).T, precision=highest)
    phase_grad = scale_factor * (cos_table * with_sin - sin_table * with_cos)
    position_grad = 2.0 * math.pi * jnp.dot(phase_grad, wave_float, precision=highest) / box
    position_grad = jnp.transpose(position_grad.reshape(BLOCKS_X, BLOCKS_Y, BLOCKS_Z, ATOMS_DEV, 3), (0, 1, 2, 4, 3))
    shape_out = (BLOCKS_X, BLOCKS_Y, BLOCKS_Z, ATOMS_DEV, CHANNEL_COUNT)
    return (updated, long_range.reshape(shape_out), charge_grad.reshape(shape_out), position_grad)
```

```python
import functools
import math

import jax
import jax.numpy as jnp
from jax import lax
from jax.experimental import pallas as pl
from jax.experimental.pallas import tpu as pltpu
from jax.sharding import PartitionSpec as P

AXES = ("gx", "gy", "gz")
cell_length = 6.8
planar_floor = 0.25
radial_width = 64.0
top_degree = 4
top_order = 2
bf16 = jnp.bfloat16
f32 = jnp.float32


def slot_of(degree, order):
    return degree * degree + degree + order


groups = [[slot_of(l, 0) for l in range(top_degree + 1)]]
for order in range(1, top_order + 1):
    groups.append([slot_of(l, sign * order) for sign in (1, -1) for l in range(order, top_degree + 1)])
slots = [slot for group in groups for slot in group]
slot_tiles = (len(slots) + 1) // 2
atom_tiles = 4


def leading(values):
    return values.astype(bf16)


def trailing(values):
    return (values - values.astype(bf16).astype(f32)).astype(bf16)


def cos_sin_turns(turns):
    rest = turns - jnp.round(turns)
    square = rest * rest
    cosine = jnp.full_like(square, cos_series[-1])
    for factor in cos_series[-2::-1]:
        cosine = cosine * square + factor
    sine = jnp.full_like(square, sin_series[-1])
    for factor in sin_series[-2::-1]:
        sine = sine * square + factor
    return cosine, sine * rest


def fitted(function, count):
    import numpy as np

    nodes = np.cos((np.arange(count) + 0.5) * np.pi / count)
    line = np.polynomial.chebyshev.chebfit(nodes, function((nodes + 1.0) / 8.0), count - 1)
    power = np.polynomial.chebyshev.cheb2poly(line)
    shift = np.polynomial.polynomial.Polynomial([-1.0, 8.0])
    total = np.polynomial.polynomial.Polynomial([0.0])
    for factor in power[::-1]:
        total = total * shift + factor
    return [float(factor) for factor in total.coef]


def _cos_of(s):
    import numpy as np

    return np.cos(2.0 * np.pi * np.sqrt(s))


def _sin_of(s):
    import numpy as np

    return np.sin(2.0 * np.pi * np.sqrt(s)) / np.sqrt(s)


cos_series = fitted(_cos_of, 8)
sin_series = fitted(_sin_of, 7)


def pack_kernel(sizes, send_ref, irreps_ref, places_ref, cotangent_ref, tiles_ref, own_ref, wide_ref):
    atoms = irreps_ref.shape[0]
    width = irreps_ref.shape[2]
    offered = send_ref.shape[0]
    wide_ref[...] = irreps_ref[...].astype(f32)
    tiles_ref[0] = wide_ref[:, 0, :].astype(bf16)
    cotangent = cotangent_ref[...]
    tiles_ref[1] = leading(cotangent)
    tiles_ref[2] = trailing(cotangent)
    lane = lax.broadcasted_iota(jnp.int32, (atoms, width), 1)
    row = lax.broadcasted_iota(jnp.int32, (atoms, atoms), 0)
    column = lax.broadcasted_iota(jnp.int32, (atoms, atoms), 1)
    packed = jnp.zeros((atoms, width), f32)
    for number, axis in enumerate(AXES):
        corner = lax.axis_index(axis).astype(f32)
        place = (places_ref[number : number + 1, :] + cell_length * corner) / jnp.float32(cell_length * sizes[number])
        standing = jnp.sum(jnp.where(row == column, place, 0.0), axis=1, keepdims=True)
        high = standing.astype(bf16).astype(f32)
        middle = (standing - high).astype(bf16).astype(f32)
        low = (standing - high) - middle
        for level, part in enumerate((high, middle, low)):
            packed = jnp.where(lane == 3 * level + number, part, packed)
    tiles_ref[3] = packed.astype(bf16)
    pick_row = lax.broadcasted_iota(jnp.int32, (offered, atoms), 0)
    pick_column = lax.broadcasted_iota(jnp.int32, (offered, atoms), 1)
    wanted = jnp.zeros((offered, atoms), jnp.int32)
    for position in range(offered):
        wanted = jnp.where(pick_row == position, send_ref[position], wanted)
    pick = jnp.where(wanted == pick_column, 1.0, 0.0).astype(bf16)
    for number, slot in enumerate(slots):
        own_ref[number] = wide_ref[:, slot, :].astype(bf16)
    for pair in range(slot_tiles):
        halves = []
        for number in (2 * pair, 2 * pair + 1):
            if number < len(slots):
                halves.append(jnp.dot(pick, own_ref[number], preferred_element_type=f32))
            else:
                halves.append(jnp.zeros((offered, width), f32))
        tiles_ref[atom_tiles + pair] = jnp.concatenate(halves, axis=0).astype(bf16)


def weight_kernel(pieces, offered, depth, neighbour_ref, displacement_ref, weights_ref):
    atoms, count = neighbour_ref.shape
    first = displacement_ref[0]
    second = displacement_ref[1]
    third = displacement_ref[2]
    planar = first * first + second * second
    radial = jnp.exp(-(planar + third * third) / radial_width) / math.sqrt(count)
    turn = planar / (planar + planar_floor)
    index = neighbour_ref[...]
    group = (index - atoms) >> (offered.bit_length() - 1)
    place = (index - atoms) & (offered - 1)
    shift_x = (group >= 9).astype(jnp.int32) + (group >= 18).astype(jnp.int32)
    group = group - 9 * shift_x
    shift_y = (group >= 3).astype(jnp.int32) + (group >= 6).astype(jnp.int32)
    shift_z = group - 3 * shift_y
    line = jnp.zeros_like(index)
    for axis, shift, reach in reversed(tuple(zip(AXES, (shift_x, shift_y, shift_z), pieces))):
        if reach == 2:
            piece = jnp.where(shift == 1, 0, 1)
        else:
            odd = lax.axis_index(axis) % 2
            piece = jnp.where(shift == 1, 0, jnp.where(shift == 2, 1 + odd, 2 - odd))
        line = line * reach + piece
    rows = jnp.where(index < atoms, index, atoms + offered * line + place)
    number = lax.broadcasted_iota(jnp.int32, (atoms, depth), 1)
    strengths = [radial, radial * turn, radial * turn * turn]
    totals = [jnp.zeros((atoms, depth), f32) for _ in strengths]
    for neighbour in range(count):
        hit = rows[:, neighbour : neighbour + 1] == number
        totals = [
            total + jnp.where(hit, strength[:, neighbour : neighbour + 1], 0.0)
            for total, strength in zip(totals, strengths)
        ]
    for order, total in enumerate(totals):
        weights_ref[2 * order * atoms : (2 * order + 1) * atoms, :] = leading(total)
        weights_ref[(2 * order + 1) * atoms : (2 * order + 2) * atoms, :] = trailing(total)


def dot_nt(left, right):
    return lax.dot_general(left, right, (((1,), (1,)), ((), ())), preferred_element_type=f32)


def main_kernel(
    sizes,
    atom_spots,
    halo_spots,
    wave_step,
    depth,
    *refs,
):
    count_in = 1 + max(spot[0] for spot in atom_spots + halo_spots)
    arrived = refs[:count_in]
    (
        own_ref,
        weights_ref,
        irreps_ref,
        cotangent_ref,
        waves_ref,
        waves_across_ref,
        filter_ref,
        zero_ref,
        one_ref,
        two_ref,
    ) = refs[count_in : count_in + 10]
    updated_ref, long_ref, charge_ref, place_ref = refs[count_in + 10 : count_in + 14]
    raw_ref, lead_ref, trail_ref, spot_ref, product_ref, table_ref, wide_ref = refs[count_in + 14 :]
    atoms, _, width = irreps_ref.shape
    waves = filter_ref.shape[0]
    total_atoms = raw_ref.shape[0]
    scale = 1.0 / math.sqrt(total_atoms * waves)

    where = 0
    for source, first, blocks in atom_spots:
        ref = arrived[source]

        def place_block(ref, start, row):
            rows = pl.ds(row, atoms)
            raw_ref[rows, :] = ref[start]
            lead_ref[rows, width:] = ref[start + 1]
            trail_ref[rows, width:] = ref[start + 2]
            spot_ref[rows, :] = ref[start + 3]

        if blocks == 1:
            place_block(ref, first, where)
        else:

            def place_many(block, carry, ref=ref, first=first, where=where):
                place_block(ref, first + block * atom_tiles, pl.multiple_of(where + block * atoms, atoms))
                return carry

            lax.fori_loop(0, blocks, place_many, 0)
        where += blocks * atoms
    charges = raw_ref[...].astype(f32)
    mean = jnp.sum(charges, axis=0, keepdims=True) / total_atoms
    centered = charges - mean
    lead_ref[:, :width] = leading(centered)
    trail_ref[:, :width] = trailing(centered)

    chunk = min(total_atoms, 512)
    mean_total = jnp.zeros((1, width), f32)
    for step in range(waves // wave_step):
        wave_rows = slice(step * wave_step, (step + 1) * wave_step)

        def add_chunk(part, carry):
            factors, plane = carry
            rows = pl.ds(pl.multiple_of(part * chunk, chunk), chunk)
            turns = dot_nt(waves_ref[wave_rows, :], spot_ref[rows, :])
            cosine, sine = cos_sin_turns(turns)
            both = jnp.concatenate([cosine, sine], axis=0)
            high = leading(both)
            low = trailing(both)
            factors = factors + (
                jnp.dot(high, lead_ref[rows, :], preferred_element_type=f32)
                + jnp.dot(high, trail_ref[rows, :], preferred_element_type=f32)
                + jnp.dot(low, lead_ref[rows, :], preferred_element_type=f32)
            )
            return factors, plane + jnp.sum(both, axis=1, keepdims=True)

        start = (jnp.zeros((2 * wave_step, 2 * width), f32), jnp.zeros((2 * wave_step, 1), f32))
        if total_atoms == chunk:
            factors, plane = add_chunk(0, start)
        else:
            factors, plane = lax.fori_loop(0, total_atoms // chunk, add_chunk, start)
        strength = filter_ref[wave_rows, :]
        strength = jnp.concatenate([strength, strength], axis=0)
        strength = jnp.concatenate([strength, strength], axis=1)
        product = strength * factors
        mean_total = mean_total + jnp.sum(plane * product[:, width:], axis=0, keepdims=True)
        product_ref[0, step] = leading(product)
        product_ref[1, step] = trailing(product)

    own_spots = spot_ref[:atoms, :]
    turns = jnp.dot(own_spots, waves_across_ref[...], preferred_element_type=f32)
    cosine, sine = cos_sin_turns(turns)
    own_charges = wide_slot(irreps_ref, 0) - mean
    pair = jnp.concatenate([cotangent_ref[...], own_charges], axis=1)
    pair = jnp.concatenate([leading(pair), trailing(pair)], axis=0)
    terms = jnp.zeros((atoms, 2 * width), f32)
    slopes = []
    for step in range(waves // wave_step):
        wave_lanes = slice(step * wave_step, (step + 1) * wave_step)
        tables = jnp.concatenate([cosine[:, wave_lanes], sine[:, wave_lanes]], axis=1)
        tables = jnp.concatenate([leading(tables), trailing(tables)], axis=0)
        high = product_ref[0, step]
        low = product_ref[1, step]
        both = jnp.dot(tables, high, preferred_element_type=f32)
        terms = terms + both[:atoms] + both[atoms:] + jnp.dot(tables[:atoms], low, preferred_element_type=f32)
        both = dot_nt(pair, high)
        against = both[:atoms] + both[atoms:] + dot_nt(pair[:atoms], low)
        slopes.append(cosine[:, wave_lanes] * against[:, wave_step:] - sine[:, wave_lanes] * against[:, :wave_step])
    long_ref[...] = scale * terms[:, :width]
    charge_ref[...] = scale * (terms[:, width:] - mean_total / total_atoms)
    slope = jnp.concatenate(slopes, axis=1)
    across = waves_across_ref[: place_rows(), :]
    pushed = dot_nt(across, leading(slope)) + dot_nt(across, trailing(slope))
    for number, size in enumerate(sizes):
        place_ref[number : number + 1, :] = (2.0 * math.pi * scale / (cell_length * size)) * pushed[number : number + 1, :]

    offered = atoms // 2
    table_ref[...] = jnp.zeros(table_ref.shape, bf16)
    for number in range(len(slots)):
        lanes = slice(number * width, (number + 1) * width)
        table_ref[:atoms, lanes] = own_ref[number]
    for first in range(0, len(halo_spots), 2):
        for tile in range(slot_tiles):
            wide = [arrived[source][start + tile].astype(f32) for source, start in halo_spots[first : first + 2]]
            if len(wide) == 1:
                wide.append(jnp.zeros((atoms, width), f32))
            for half in range(2):
                number = 2 * tile + half
                if number < len(slots):
                    rows = slice(half * offered, (half + 1) * offered)
                    table_ref[
                        atoms + first * offered : atoms + (first + 2) * offered, number * width : (number + 1) * width
                    ] = jnp.concatenate([wide[0][rows], wide[1][rows]], axis=0).astype(bf16)
    outputs = {}
    lane = 0
    for order, (group, mixing_ref) in enumerate(zip(groups, (zero_ref, one_ref, two_ref))):
        span = len(group) * width
        both = jnp.dot(
            weights_ref[2 * order * atoms : 2 * (order + 1) * atoms, :],
            table_ref[:, lane : lane + span],
            preferred_element_type=f32,
        )
        lane += span
        gathered = both[:atoms] + both[atoms:]
        if order == 0:
            both = jnp.dot(
                jnp.concatenate([leading(gathered), trailing(gathered)], axis=0),
                mixing_ref[...],
                preferred_element_type=f32,
            )
            mixed = both[:atoms] + both[atoms:]
        else:
            half = span // 2
            plus, minus = gathered[:, :half], gathered[:, half:]
            both = jnp.dot(
                jnp.concatenate([leading(plus), leading(minus), trailing(plus), trailing(minus)], axis=0),
                mixing_ref[...],
                preferred_element_type=f32,
            )
            both = both[: 2 * atoms] + both[2 * atoms :]
            mixed = jnp.concatenate(
                [both[:atoms, :half] - both[atoms:, half:], both[atoms:, :half] + both[:atoms, half:]], axis=1
            )
        for number, slot in enumerate(group):
            outputs[slot] = mixed[:, number * width : (number + 1) * width]
    wide_ref[...] = irreps_ref[...].astype(f32)
    for slot, message in outputs.items():
        wide_ref[:, slot, :] = wide_ref[:, slot, :] + message
    updated_ref[...] = wide_ref[...].astype(bf16)


def place_rows():
    return 16


def wide_slot(irreps_ref, slot):
    return irreps_ref[:, slot, :].astype(f32)


def swap(value, sizes, partner):
    perm = []
    for x in range(sizes[0]):
        for y in range(sizes[1]):
            for z in range(sizes[2]):
                a, b, c = partner(x, y, z)
                perm.append(((x * sizes[1] + y) * sizes[2] + z, (a * sizes[1] + b) * sizes[2] + c))
    return lax.ppermute(value, AXES, perm)


def pair_of(index, size):
    return index ^ 1


def other_of(index, size):
    return (index - 1) % size if index % 2 == 0 else (index + 1) % size


def exchange(tiles, sizes):
    size_x, size_y, size_z = sizes
    block = tiles.shape[0]
    halo_start = atom_tiles
    if size_x == 4 and size_y == 4 and size_z == 2:
        paired = swap(tiles, sizes, lambda x, y, z: (x ^ 1, y, z))
        crossed = swap(jnp.concatenate([tiles[:atom_tiles], paired]), sizes, lambda x, y, z: (x ^ 2, y, z))
        line = jnp.concatenate([tiles, paired, crossed])
        by_y = swap(line, sizes, lambda x, y, z: (x, y ^ 3, z))
        by_z = swap(line, sizes, lambda x, y, z: (x, y, z ^ 1))
        by_both = swap(line, sizes, lambda x, y, z: (x, y ^ 3, z ^ 1))
        mine = [line, by_y, by_z, by_both]
        theirs = [swap(part, sizes, lambda x, y, z: (x, y ^ 1, z)) for part in mine]
        arrays = mine + theirs
        atom_spots = []
        for number in range(len(arrays)):
            for first in (0, block, 2 * block, 2 * block + atom_tiles):
                atom_spots.append((number, first, 1))
        line_spots = (halo_start, block + halo_start, 2 * block + 2 * atom_tiles)
        halo_spots = [(number, first) for number in (0, 4, 1, 2, 6, 3) for first in line_spots]
        return arrays, atom_spots, halo_spots
    everyone = lax.all_gather(tiles[:atom_tiles], AXES, axis=0, tiled=True)
    layers = [tiles[atom_tiles:]]
    for number in range(3):
        arrived = []
        for partner in (pair_of, other_of)[: 1 if sizes[number] == 2 else 2]:

            def step(*place, number=number, partner=partner):
                place = list(place)
                place[number] = partner(place[number], sizes[number])
                return place

            arrived += [swap(part, sizes, step) for part in layers]
        layers = layers + arrived
    arrays = [tiles, everyone] + layers[1:]
    blocks = size_x * size_y * size_z
    atom_spots = [(1, 0, blocks)]
    halo_spots = [(0, halo_start)] + [(2 + number, 0) for number in range(len(layers) - 1)]
    return arrays, atom_spots, halo_spots


def vmem():
    return pl.BlockSpec(memory_space=pltpu.VMEM)


def local(
    node_irreps,
    positions,
    send_list,
    neighbours,
    displacements,
    order_zero,
    order_one,
    order_two,
    reciprocal_triples,
    reciprocal_filter,
    cotangent,
):
    sizes = tuple(lax.axis_size(axis) for axis in AXES)
    irreps = node_irreps[0, 0, 0]
    atoms, harmonics, width = irreps.shape
    sent = send_list[0, 0, 0]
    offered = sent.shape[0]
    neighbour = neighbours[0, 0, 0]
    count = neighbour.shape[1]
    waves = reciprocal_filter.shape[0]
    total_atoms = atoms * math.prod(sizes)
    own_cotangent = cotangent[0, 0, 0]

    tiles, own = pl.pallas_call(
        functools.partial(pack_kernel, sizes),
        out_shape=(
            jax.ShapeDtypeStruct((atom_tiles + slot_tiles, atoms, width), bf16),
            jax.ShapeDtypeStruct((len(slots), atoms, width), bf16),
        ),
        in_specs=[pl.BlockSpec(memory_space=pltpu.SMEM), vmem(), vmem(), vmem()],
        out_specs=(vmem(), vmem()),
        scratch_shapes=[pltpu.VMEM((atoms, harmonics, width), f32)],
        name="pack",
    )(sent, irreps, positions[0, 0, 0], own_cotangent)

    arrays, atom_spots, halo_spots = exchange(tiles, sizes)
    if atom_spots[0][0] == 1:
        atom_spots, arrays = own_first(arrays, atom_spots)
    pieces = tuple(2 if size == 2 else 3 for size in sizes)
    depth = -(-(atoms + offered * math.prod(pieces)) // 256) * 256

    weights = pl.pallas_call(
        functools.partial(weight_kernel, pieces, offered, depth),
        out_shape=jax.ShapeDtypeStruct((2 * len(groups) * atoms, depth), bf16),
        in_specs=[vmem(), vmem()],
        out_specs=vmem(),
        name="weights",
    )(neighbour, displacements[0, 0, 0].reshape(3, atoms, count))

    triples = reciprocal_triples.astype(bf16)
    spread = jnp.concatenate([triples] * 3 + [jnp.zeros((waves, width - 9), bf16)], axis=1)
    wave_step = 128
    outs = pl.pallas_call(
        functools.partial(main_kernel, sizes, tuple(atom_spots), tuple(halo_spots), wave_step, depth),
        out_shape=(
            jax.ShapeDtypeStruct((atoms, harmonics, width), bf16),
            jax.ShapeDtypeStruct((atoms, width), f32),
            jax.ShapeDtypeStruct((atoms, width), f32),
            jax.ShapeDtypeStruct((3, atoms), f32),
        ),
        in_specs=[vmem() for _ in range(len(arrays) + 10)],
        out_specs=tuple(vmem() for _ in range(4)),
        scratch_shapes=[
            pltpu.VMEM((total_atoms, width), bf16),
            pltpu.VMEM((total_atoms, 2 * width), bf16),
            pltpu.VMEM((total_atoms, 2 * width), bf16),
            pltpu.VMEM((total_atoms, width), bf16),
            pltpu.VMEM((2, waves // wave_step, 2 * wave_step, 2 * width), bf16),
            pltpu.VMEM((depth, len(slots) * width), bf16),
            pltpu.VMEM((atoms, harmonics, width), f32),
        ],
        name="main",
    )(
        *arrays,
        own,
        weights,
        irreps,
        own_cotangent,
        spread,
        spread.T,
        reciprocal_filter,
        order_zero,
        order_one,
        order_two,
    )
    return tuple(out[None, None, None] for out in outs)


def own_first(arrays, atom_spots):
    me = lax.axis_index(AXES)
    everyone = jnp.roll(arrays[1], -me * atom_tiles, axis=0)
    return atom_spots, [arrays[0], everyone] + arrays[2:]


def solution(mesh):
    return jax.shard_map(
        local,
        mesh=mesh,
        in_specs=(
            P("gx", "gy", "gz", None, None, None),
            P("gx", "gy", "gz", None, None),
            P("gx", "gy", "gz", None),
            P("gx", "gy", "gz", None, None),
            P("gx", "gy", "gz", None, None),
            P(),
            P(),
            P(),
            P(),
            P(),
            P("gx", "gy", "gz", None, None),
        ),
        out_specs=(
            P("gx", "gy", "gz", None, None, None),
            P("gx", "gy", "gz", None, None),
            P("gx", "gy", "gz", None, None),
            P("gx", "gy", "gz", None, None),
        ),
        check_vma=False,
    )
```

```python
import functools
import math

import jax
import jax.numpy as jnp
from jax import lax
from jax.experimental import pallas as pl
from jax.experimental.pallas import tpu as pltpu
from jax.sharding import PartitionSpec as P


AXES = ("gx", "gy", "gz")
cell_length = 6.8
planar_floor = 0.25
radial_width = 64.0
top_degree = 4
top_order = 2
bf16 = jnp.bfloat16
f32 = jnp.float32


def slot_of(degree, order):
    return degree * degree + degree + order


groups = [[slot_of(l, 0) for l in range(top_degree + 1)]]
for order in range(1, top_order + 1):
    groups.append([slot_of(l, sign * order) for sign in (1, -1) for l in range(order, top_degree + 1)])
slots = [slot for group in groups for slot in group]
slot_tiles = (len(slots) + 1) // 2
atom_tiles = 4


def leading(values):
    return values.astype(bf16)


def trailing(values):
    return (values - values.astype(bf16).astype(f32)).astype(bf16)


def cos_sin_turns(turns):
    rest = turns - jnp.round(turns)
    square = rest * rest
    cosine = jnp.full_like(square, cos_series[-1])
    for factor in cos_series[-2::-1]:
        cosine = cosine * square + factor
    sine = jnp.full_like(square, sin_series[-1])
    for factor in sin_series[-2::-1]:
        sine = sine * square + factor
    return cosine, sine * rest


def fitted(function, count):
    import numpy as np

    nodes = np.cos((np.arange(count) + 0.5) * np.pi / count)
    line = np.polynomial.chebyshev.chebfit(nodes, function((nodes + 1.0) / 8.0), count - 1)
    power = np.polynomial.chebyshev.cheb2poly(line)
    shift = np.polynomial.polynomial.Polynomial([-1.0, 8.0])
    total = np.polynomial.polynomial.Polynomial([0.0])
    for factor in power[::-1]:
        total = total * shift + factor
    return [float(factor) for factor in total.coef]


def _cos_of(s):
    import numpy as np

    return np.cos(2.0 * np.pi * np.sqrt(s))


def _sin_of(s):
    import numpy as np

    return np.sin(2.0 * np.pi * np.sqrt(s)) / np.sqrt(s)


cos_series = fitted(_cos_of, 7)
sin_series = fitted(_sin_of, 6)


def standing_row(row):
    count = row.shape[1]
    down = lax.broadcasted_iota(jnp.int32, (count, count), 0)
    across = lax.broadcasted_iota(jnp.int32, (count, count), 1)
    return jnp.sum(jnp.where(down == across, row, 0.0), axis=1, keepdims=True)


def lying_column(column):
    count = column.shape[0]
    down = lax.broadcasted_iota(jnp.int32, (count, count), 0)
    across = lax.broadcasted_iota(jnp.int32, (count, count), 1)
    return jnp.sum(jnp.where(down == across, column, 0.0), axis=0, keepdims=True)


def dot(left, right):
    return jnp.dot(left, right, preferred_element_type=f32)


def dot_nt(left, right):
    return lax.dot_general(left, right, (((1,), (1,)), ((), ())), preferred_element_type=f32)


def pack_kernel(sizes, *refs):
    far = refs[:4]
    tiles_ref = refs[4]
    near_refs = refs[5:9]
    arrivals = refs[9]
    copies = [pltpu.make_async_copy(a, b, arrivals.at[i]) for i, (a, b) in enumerate(zip(far, near_refs))]
    for copy in copies:
        copy.start()
    for copy in copies:
        copy.wait()
    send_ref, irreps_ref, places_ref, cotangent_ref = near_refs
    _, atoms, width = irreps_ref.shape
    offered = send_ref.shape[0]
    tiles_ref[0] = irreps_ref[0]
    cotangent = cotangent_ref[...]
    tiles_ref[1] = leading(cotangent)
    tiles_ref[2] = trailing(cotangent)
    lane = lax.broadcasted_iota(jnp.int32, (atoms, width), 1)
    packed = jnp.zeros((atoms, width), f32)
    for number, axis in enumerate(AXES):
        corner = lax.axis_index(axis).astype(f32)
        place = (places_ref[number] + cell_length * corner) / jnp.float32(cell_length * sizes[number])
        place = standing_row(place)
        high = place.astype(bf16).astype(f32)
        middle = (place - high).astype(bf16).astype(f32)
        low = (place - high) - middle
        for level, part in enumerate((high, middle, low)):
            packed = jnp.where(lane == 3 * level + number, part, packed)
    tiles_ref[3] = packed.astype(bf16)
    pick_row = lax.broadcasted_iota(jnp.int32, (offered, atoms), 0)
    pick_column = lax.broadcasted_iota(jnp.int32, (offered, atoms), 1)
    wanted = jnp.zeros((offered, atoms), jnp.int32)
    for position in range(offered):
        wanted = jnp.where(pick_row == position, send_ref[position], wanted)
    pick = jnp.where(wanted == pick_column, 1.0, 0.0).astype(bf16)
    rows = dot(pick, jnp.concatenate([irreps_ref[slot] for slot in slots], axis=1))
    for pair in range(slot_tiles):
        halves = []
        for number in (2 * pair, 2 * pair + 1):
            if number < len(slots):
                halves.append(rows[:, number * width : (number + 1) * width])
            else:
                halves.append(jnp.zeros((offered, width), f32))
        tiles_ref[atom_tiles + pair] = jnp.concatenate(halves, axis=0).astype(bf16)


def prepare_kernel(
    pieces, offered, neighbour_ref, displacement_ref, triples_ref, far_filter_ref, weights_ref, waves_ref, filter_ref, arrival
):
    waves = filter_ref.shape[0]
    shares = far_filter_ref.shape[0] // waves
    first_wave = pl.multiple_of((lax.axis_index("gy") % shares) * waves, waves)
    filter_copy = pltpu.make_async_copy(far_filter_ref.at[pl.ds(first_wave, waves), :], filter_ref, arrival)
    filter_copy.start()
    atoms, count = neighbour_ref.shape
    edges = atoms * count
    depth = weights_ref.shape[1]
    width = waves_ref.shape[1]
    first = displacement_ref[0]
    second = displacement_ref[1]
    third = displacement_ref[2]
    planar = first * first + second * second
    radial = jnp.exp(-(planar + third * third) / radial_width) / math.sqrt(count)
    turn = planar / (planar + planar_floor)
    slot = lax.broadcasted_iota(jnp.int32, (count, edges), 0)
    edge = lax.broadcasted_iota(jnp.int32, (count, edges), 1)
    repeat = jnp.where(edge % count == slot, 1.0, 0.0)
    spread = jnp.dot(
        neighbour_ref[...].astype(f32), repeat, precision=lax.Precision.HIGHEST, preferred_element_type=f32
    )
    owner = lax.broadcasted_iota(jnp.int32, (atoms, edges), 0)
    mine = owner == lax.broadcasted_iota(jnp.int32, (atoms, edges), 1) // count
    index = jnp.sum(jnp.where(mine, spread, 0.0), axis=0, keepdims=True).astype(jnp.int32)
    group = (index - atoms) // offered
    place = (index - atoms) - offered * group
    shift_x = (group >= 9).astype(jnp.int32) + (group >= 18).astype(jnp.int32)
    group = group - 9 * shift_x
    shift_y = (group >= 3).astype(jnp.int32) + (group >= 6).astype(jnp.int32)
    shift_z = group - 3 * shift_y
    line = jnp.zeros_like(index)
    for axis, shift, reach in reversed(tuple(zip(AXES, (shift_x, shift_y, shift_z), pieces))):
        if reach == 2:
            piece = jnp.where(shift == 1, 0, 1)
        else:
            odd = lax.axis_index(axis) % 2
            piece = jnp.where(shift == 1, 0, jnp.where(shift == 2, 1 + odd, 2 - odd))
        line = line * reach + piece
    rows = jnp.where(index < atoms, index, atoms + offered * line + place)
    hits = jnp.where(rows == lax.broadcasted_iota(jnp.int32, (depth, edges), 0), 1.0, 0.0).astype(bf16)
    strengths = [jnp.where(mine, strength, 0.0) for strength in (radial, radial * turn, radial * turn * turn)]
    strengths = jnp.concatenate(strengths, axis=0)
    both = dot_nt(jnp.concatenate([leading(strengths), trailing(strengths)], axis=0), hits)
    total = both[: len(groups) * atoms] + both[len(groups) * atoms :]
    for order in range(len(groups)):
        part = total[order * atoms : (order + 1) * atoms]
        weights_ref[2 * order * atoms : 2 * (order + 1) * atoms, :] = jnp.concatenate(
            [leading(part), trailing(part)], axis=0
        )
    triples = triples_ref[:, pl.ds(first_wave, waves)].astype(f32)
    triples = jnp.concatenate([triples, jnp.zeros((5, triples.shape[1]), f32)], axis=0)
    component = lax.broadcasted_iota(jnp.int32, (8, width), 0)
    lane = lax.broadcasted_iota(jnp.int32, (8, width), 1)
    chosen = jnp.where((lane % 3 == component) & (lane < 9), 1.0, 0.0)
    waves_ref[...] = lax.dot_general(
        triples.astype(bf16), chosen.astype(bf16), (((0,), (0,)), ((), ())), preferred_element_type=f32
    ).astype(bf16)
    filter_copy.wait()


def ewald_kernel(atom_spots, recipients, shares, wave_step, *refs):
    count_in = 1 + max(spot[0] for spot in atom_spots)
    arrived = refs[:count_in]
    waves_ref, filter_ref = refs[count_in : count_in + 2]
    part_refs = refs[count_in + 2 : count_in + 2 + shares]
    raw_ref, lead_ref, trail_ref, spot_ref, product_ref = refs[count_in + 2 + shares :]
    atoms, width = arrived[0].shape[1:]
    waves = filter_ref.shape[0]
    total_atoms = raw_ref.shape[0]

    where = 0
    for source, first, blocks in atom_spots:
        ref = arrived[source]

        def place_block(ref, start, row):
            rows = pl.ds(row, atoms)
            raw_ref[rows, :] = ref[start]
            lead_ref[rows, width:] = ref[start + 1]
            trail_ref[rows, width:] = ref[start + 2]
            spot_ref[rows, :] = ref[start + 3]

        if blocks <= 32:
            for block in range(blocks):
                place_block(ref, first + block * atom_tiles, where + block * atoms)
        else:

            def place_many(block, carry, ref=ref, first=first, where=where):
                place_block(ref, first + block * atom_tiles, pl.multiple_of(where + block * atoms, atoms))
                return carry

            lax.fori_loop(0, blocks, place_many, 0)
        where += blocks * atoms
    charges = raw_ref[...].astype(f32)
    mean = jnp.sum(charges, axis=0, keepdims=True) / total_atoms
    centered = charges - mean
    lead_ref[:, :width] = leading(centered)
    trail_ref[:, :width] = trailing(centered)

    def wave_rows(step):
        return slice(step * wave_step, (step + 1) * wave_step)

    chunk = min(total_atoms, 512)
    mean_total = jnp.zeros((1, width), f32)
    for step in range(waves // wave_step):

        def add_chunk(part, carry):
            factors, plane = carry
            rows = pl.ds(part * chunk, chunk) if isinstance(part, int) else pl.ds(pl.multiple_of(part * chunk, chunk), chunk)
            turns = dot_nt(waves_ref[wave_rows(step), :], spot_ref[rows, :])
            cosine, sine = cos_sin_turns(turns)
            both = jnp.concatenate([cosine, sine], axis=0)
            high = leading(both)
            low = trailing(both)
            factors = factors + (
                dot(high, lead_ref[rows, :]) + dot(high, trail_ref[rows, :]) + dot(low, lead_ref[rows, :])
            )
            return factors, plane + jnp.sum(both, axis=1, keepdims=True)

        start = (jnp.zeros((2 * wave_step, 2 * width), f32), jnp.zeros((2 * wave_step, 1), f32))
        if total_atoms == chunk:
            factors, plane = add_chunk(0, start)
        else:
            factors, plane = lax.fori_loop(0, total_atoms // chunk, add_chunk, start)
        strength = filter_ref[wave_rows(step), :]
        strength = jnp.concatenate([strength, strength], axis=0)
        strength = jnp.concatenate([strength, strength], axis=1)
        product = strength * factors
        mean_total = mean_total + jnp.sum(plane * product[:, width:], axis=0, keepdims=True)
        product_ref[0, step] = leading(product)
        product_ref[1, step] = trailing(product)

    def of_recipients(ref):
        return jnp.concatenate([ref[row : row + atoms, :] for row in recipients], axis=0)

    count = shares * atoms
    spots = of_recipients(spot_ref)
    swapped = []
    for ref in (lead_ref, trail_ref):
        pair = of_recipients(ref)
        swapped.append(jnp.concatenate([pair[:, width:], pair[:, :width]], axis=1))
    pair = jnp.concatenate(swapped, axis=0)
    terms = jnp.zeros((count, 2 * width), f32)
    pushed = jnp.zeros((2 * count, width), f32)
    for step in range(waves // wave_step):
        cosine, sine = cos_sin_turns(dot_nt(spots, waves_ref[wave_rows(step), :]))
        tables = jnp.concatenate([cosine, sine], axis=1)
        tables = jnp.concatenate([leading(tables), trailing(tables)], axis=0)
        high = product_ref[0, step]
        low = product_ref[1, step]
        both = dot(tables, high)
        terms = terms + both[:count] + both[count:] + dot(tables[:count], low)
        both = dot_nt(pair, high)
        against = both[:count] + both[count:] + dot_nt(pair[:count], low)
        slope = cosine * against[:, wave_step:] - sine * against[:, :wave_step]
        slope = jnp.concatenate([leading(slope), trailing(slope)], axis=0)
        pushed = pushed + dot(slope, waves_ref[wave_rows(step), :])
    charge = terms[:, width:] - mean_total / total_atoms
    pushed = pushed[:count] + pushed[count:]
    for number, ref in enumerate(part_refs):
        rows = slice(number * atoms, (number + 1) * atoms)
        ref[0] = terms[rows, :width]
        ref[1] = charge[rows]
        ref[2] = pushed[rows]


def edge_kernel(sizes, scale, halo_spots, part_count, *refs):
    count_in = 1 + max(spot[0] for spot in halo_spots)
    arrived = refs[:count_in]
    part_refs = refs[count_in : count_in + part_count]
    irreps_ref, weights_ref, zero_ref, one_ref, two_ref = refs[count_in + part_count : count_in + part_count + 5]
    updated_ref, long_ref, charge_ref, place_ref, table_ref = refs[count_in + part_count + 5 :]
    harmonics, atoms, width = irreps_ref.shape
    offered = atoms // 2

    sums = []
    for number in range(3):
        total = part_refs[0][number]
        for ref in part_refs[1:]:
            total = total + ref[number]
        sums.append(scale * total)
    long_ref[...] = sums[0]
    charge_ref[...] = sums[1]
    for number, size in enumerate(sizes):
        factor = 2.0 * math.pi / (cell_length * size)
        place_ref[number] = factor * lying_column(sums[2][:, number : number + 1])

    used = atoms + offered * len(halo_spots)
    if len(halo_spots) % 2:
        used -= offered
    table_ref[used:, :] = jnp.zeros((table_ref.shape[0] - used, table_ref.shape[1]), bf16)
    for number, slot in enumerate(slots):
        table_ref[:atoms, number * width : (number + 1) * width] = irreps_ref[slot]
    for first in range(0, len(halo_spots), 2):
        for tile in range(slot_tiles):
            wide = [arrived[source][start + tile].astype(f32) for source, start in halo_spots[first : first + 2]]
            if len(wide) == 1:
                wide.append(jnp.zeros((atoms, width), f32))
            for half in range(2):
                number = 2 * tile + half
                if number < len(slots):
                    rows = slice(half * offered, (half + 1) * offered)
                    table_ref[
                        atoms + first * offered : atoms + (first + 2) * offered, number * width : (number + 1) * width
                    ] = jnp.concatenate([wide[0][rows], wide[1][rows]], axis=0).astype(bf16)
    outputs = {}
    lane = 0
    for order, (group, mixing_ref) in enumerate(zip(groups, (zero_ref, one_ref, two_ref))):
        span = len(group) * width
        both = dot(weights_ref[2 * order * atoms : 2 * (order + 1) * atoms, :], table_ref[:, lane : lane + span])
        lane += span
        gathered = both[:atoms] + both[atoms:]
        if order == 0:
            both = dot(jnp.concatenate([leading(gathered), trailing(gathered)], axis=0), mixing_ref[...])
            mixed = both[:atoms] + both[atoms:]
        else:
            half = span // 2
            plus, minus = gathered[:, :half], gathered[:, half:]
            both = dot(
                jnp.concatenate([leading(plus), leading(minus), trailing(plus), trailing(minus)], axis=0),
                mixing_ref[...],
            )
            both = both[: 2 * atoms] + both[2 * atoms :]
            mixed = jnp.concatenate(
                [both[:atoms, :half] - both[atoms:, half:], both[atoms:, :half] + both[:atoms, half:]], axis=1
            )
        for number, slot in enumerate(group):
            outputs[slot] = mixed[:, number * width : (number + 1) * width]
    for slot in range(harmonics):
        if slot in outputs:
            updated_ref[slot] = (irreps_ref[slot].astype(f32) + outputs[slot]).astype(bf16)
        else:
            updated_ref[slot] = irreps_ref[slot]


def swap(value, sizes, partner):
    perm = []
    for x in range(sizes[0]):
        for y in range(sizes[1]):
            for z in range(sizes[2]):
                a, b, c = partner(x, y, z)
                perm.append(((x * sizes[1] + y) * sizes[2] + z, (a * sizes[1] + b) * sizes[2] + c))
    return lax.ppermute(value, AXES, perm)


def pair_of(index, size):
    return index ^ 1


def other_of(index, size):
    return (index - 1) % size if index % 2 == 0 else (index + 1) % size


def exchange(tiles, sizes):
    size_x, size_y, size_z = sizes
    if size_x == 4 and size_y == 4 and size_z == 2:
        paired = swap(tiles, sizes, lambda x, y, z: (x ^ 1, y, z))
        crossed = swap(jnp.concatenate([tiles[:atom_tiles], paired]), sizes, lambda x, y, z: (x ^ 2, y, z))
        atoms = jnp.concatenate([tiles[:atom_tiles], paired[:atom_tiles], crossed[: 2 * atom_tiles]])
        halo = jnp.concatenate([tiles[atom_tiles:], paired[atom_tiles:], crossed[2 * atom_tiles :]])

        def by_y(x, y, z):
            return (x, y ^ 3, z)

        def by_z(x, y, z):
            return (x, y, z ^ 1)

        def by_both(x, y, z):
            return (x, y ^ 3, z ^ 1)

        def by_core(x, y, z):
            return (x, y ^ 1, z)

        far = [swap(atoms, sizes, by_y), swap(atoms, sizes, by_z)]
        far = jnp.concatenate(far + [swap(atoms, sizes, by_both)])
        atom_arrays = [atoms, far, swap(atoms, sizes, by_core), swap(far, sizes, by_core)]
        halo_y = swap(halo, sizes, by_y)
        halo_z = swap(halo, sizes, by_z)
        halo_both = swap(halo, sizes, by_both)
        halo_core = swap(halo, sizes, by_core)
        halo_z_core = swap(halo_z, sizes, by_core)
        halo_arrays = [halo, halo_core, halo_y, halo_z, halo_z_core, halo_both]
        atom_spots = [(number, 0, array.shape[0] // atom_tiles) for number, array in enumerate(atom_arrays)]
        halo_spots = [(number, slot_tiles * piece) for number in range(6) for piece in range(3)]
        total_rows = sum(spot[2] for spot in atom_spots) * tiles.shape[1]
        return atom_arrays, atom_spots, halo_arrays, halo_spots, (0, total_rows // 2)
    everyone = lax.all_gather(tiles[:atom_tiles], AXES, axis=0, tiled=True)
    everyone = jnp.roll(everyone, -lax.axis_index(AXES) * atom_tiles, axis=0)
    layers = [tiles[atom_tiles:]]
    for number in range(3):
        arrived = []
        for partner in (pair_of, other_of)[: 1 if sizes[number] == 2 else 2]:

            def step(*place, number=number, partner=partner):
                place = list(place)
                place[number] = partner(place[number], sizes[number])
                return place

            arrived += [swap(part, sizes, step) for part in layers]
        layers = layers + arrived
    return [everyone], [(0, 0, math.prod(sizes))], layers, [(number, 0) for number in range(len(layers))], (0,)


def vmem():
    return pl.BlockSpec(memory_space=pltpu.VMEM)


def far():
    return pl.BlockSpec(memory_space=pltpu.HBM)


def grant(mebibytes):
    return pltpu.CompilerParams(vmem_limit_bytes=mebibytes * 2**20)


def stay(value):
    return pltpu.with_memory_space_constraint(value, pltpu.HBM)


def near(value):
    return pltpu.with_memory_space_constraint(value, pltpu.VMEM)


def layer(
    node_irreps,
    positions,
    send_list,
    neighbours,
    displacements,
    order_zero,
    order_one,
    order_two,
    reciprocal_triples,
    reciprocal_filter,
    cotangent,
):
    sizes = tuple(lax.axis_size(axis) for axis in AXES)
    irreps = jnp.transpose(node_irreps[0, 0, 0], (1, 0, 2))
    harmonics, atoms, width = irreps.shape
    sent = send_list[0, 0, 0]
    offered = sent.shape[0]
    neighbour = neighbours[0, 0, 0]
    waves = reciprocal_filter.shape[0]
    total_atoms = atoms * math.prod(sizes)
    own_cotangent = cotangent[0, 0, 0]

    tiles = pl.pallas_call(
        functools.partial(pack_kernel, sizes),
        out_shape=jax.ShapeDtypeStruct((atom_tiles + slot_tiles, atoms, width), bf16),
        in_specs=[far() for _ in range(4)],
        out_specs=vmem(),
        scratch_shapes=[
            pltpu.SMEM(sent.shape, jnp.int32),
            pltpu.VMEM(irreps.shape, bf16),
            pltpu.VMEM((3, 1, atoms), f32),
            pltpu.VMEM(own_cotangent.shape, f32),
            pltpu.SemaphoreType.DMA((4,)),
        ],
        compiler_params=grant(4),
        name="pack",
    )(*map(stay, (sent, irreps, positions[0, 0, 0][:, None, :], own_cotangent)))

    atom_arrays, atom_spots, halo_arrays, halo_spots, recipients = exchange(tiles, sizes)
    shares = len(recipients)
    pieces = tuple(2 if size == 2 else 3 for size in sizes)
    depth = -(-(atoms + offered * math.prod(pieces)) // 256) * 256

    weights, spread, strengths = pl.pallas_call(
        functools.partial(prepare_kernel, pieces, offered),
        out_shape=(
            jax.ShapeDtypeStruct((2 * len(groups) * atoms, depth), bf16),
            jax.ShapeDtypeStruct((waves // shares, width), bf16),
            jax.ShapeDtypeStruct((waves // shares, width), f32),
        ),
        in_specs=[vmem(), vmem(), vmem(), far()],
        out_specs=(vmem(), vmem(), vmem()),
        scratch_shapes=[pltpu.SemaphoreType.DMA],
        compiler_params=grant(6),
        name="prepare",
    )(
        *map(near, (neighbour, displacements[0, 0, 0][:, None, :], reciprocal_triples.T)), stay(reciprocal_filter)
    )

    wave_step = 128
    part_shape = jax.ShapeDtypeStruct((3, atoms, width), f32)
    parts = pl.pallas_call(
        functools.partial(ewald_kernel, tuple(atom_spots), recipients, shares, wave_step),
        out_shape=[part_shape] * shares,
        in_specs=[vmem() for _ in range(len(atom_arrays) + 2)],
        out_specs=[vmem()] * shares,
        scratch_shapes=[
            pltpu.VMEM((total_atoms, width), bf16),
            pltpu.VMEM((total_atoms, 2 * width), bf16),
            pltpu.VMEM((total_atoms, 2 * width), bf16),
            pltpu.VMEM((total_atoms, width), bf16),
            pltpu.VMEM((2, waves // shares // wave_step, 2 * wave_step, 2 * width), bf16),
        ],
        compiler_params=grant(12 + total_atoms // 256),
        name="ewald",
    )(*map(near, (*atom_arrays, spread, strengths)))
    parts = list(parts)
    if shares > 1:
        parts[1] = swap(parts[1], sizes, lambda x, y, z: (x, y ^ 1, z))

    scale = 1.0 / math.sqrt(total_atoms * waves)
    updated, long_range, charge_grad, position_grad = pl.pallas_call(
        functools.partial(edge_kernel, sizes, scale, tuple(halo_spots), shares),
        out_shape=(
            jax.ShapeDtypeStruct((harmonics, atoms, width), bf16),
            jax.ShapeDtypeStruct((atoms, width), f32),
            jax.ShapeDtypeStruct((atoms, width), f32),
            jax.ShapeDtypeStruct((3, 1, atoms), f32),
        ),
        in_specs=[vmem() for _ in range(len(halo_arrays) + shares + 5)],
        out_specs=tuple(vmem() for _ in range(4)),
        scratch_shapes=[pltpu.VMEM((depth, len(slots) * width), bf16)],
        compiler_params=grant(12),
        name="edges",
    )(*map(near, (*halo_arrays, *parts, irreps, weights, order_zero, order_one, order_two)))
    outs = (jnp.transpose(updated, (1, 0, 2)), long_range, charge_grad, position_grad[:, 0, :])
    return tuple(out[None, None, None] for out in outs)


def solution(mesh):
    return jax.shard_map(
        layer,
        mesh=mesh,
        in_specs=(
            P("gx", "gy", "gz", None, None, None),
            P("gx", "gy", "gz", None, None),
            P("gx", "gy", "gz", None),
            P("gx", "gy", "gz", None, None),
            P("gx", "gy", "gz", None, None),
            P(),
            P(),
            P(),
            P(),
            P(),
            P("gx", "gy", "gz", None, None),
        ),
        out_specs=(
            P("gx", "gy", "gz", None, None, None),
            P("gx", "gy", "gz", None, None),
            P("gx", "gy", "gz", None, None),
            P("gx", "gy", "gz", None, None),
        ),
        check_vma=False,
    )
```

```python
import functools
import math

import jax
import jax.numpy as jnp
from jax import lax
from jax.experimental import pallas as pl
from jax.experimental.pallas import tpu as pltpu
from jax.sharding import PartitionSpec as P


AXES = ("gx", "gy", "gz")
cell_length = 6.8
planar_floor = 0.25
radial_width = 64.0
top_degree = 4
top_order = 2
bf16 = jnp.bfloat16
f32 = jnp.float32


def slot_of(degree, order):
    return degree * degree + degree + order


groups = [[slot_of(l, 0) for l in range(top_degree + 1)]]
for order in range(1, top_order + 1):
    groups.append([slot_of(l, sign * order) for sign in (1, -1) for l in range(order, top_degree + 1)])
slots = [slot for group in groups for slot in group]
slot_tiles = len(slots) // 2
atom_tiles = 4
place_lanes = 16


def leading(values):
    return values.astype(bf16)


def trailing(values):
    return (values - values.astype(bf16).astype(f32)).astype(bf16)


def cos_sin_turns(turns):
    rest = turns - jnp.round(turns)
    square = rest * rest
    cosine = jnp.full_like(square, cos_series[-1])
    for factor in cos_series[-2::-1]:
        cosine = cosine * square + factor
    sine = jnp.full_like(square, sin_series[-1])
    for factor in sin_series[-2::-1]:
        sine = sine * square + factor
    return cosine, sine * rest


def fitted(function, count):
    import numpy as np

    nodes = np.cos((np.arange(count) + 0.5) * np.pi / count)
    line = np.polynomial.chebyshev.chebfit(nodes, function((nodes + 1.0) / 8.0), count - 1)
    power = np.polynomial.chebyshev.cheb2poly(line)
    shift = np.polynomial.polynomial.Polynomial([-1.0, 8.0])
    total = np.polynomial.polynomial.Polynomial([0.0])
    for factor in power[::-1]:
        total = total * shift + factor
    return [float(factor) for factor in total.coef]


def _cos_of(s):
    import numpy as np

    return np.cos(2.0 * np.pi * np.sqrt(s))


def _sin_of(s):
    import numpy as np

    return np.sin(2.0 * np.pi * np.sqrt(s)) / np.sqrt(s)


cos_series = fitted(_cos_of, 7)
sin_series = fitted(_sin_of, 6)


def standing_row(row):
    count = row.shape[1]
    down = lax.broadcasted_iota(jnp.int32, (count, count), 0)
    across = lax.broadcasted_iota(jnp.int32, (count, count), 1)
    return jnp.sum(jnp.where(down == across, row, 0.0), axis=1, keepdims=True)


def lying_column(column):
    count = column.shape[0]
    down = lax.broadcasted_iota(jnp.int32, (count, count), 0)
    across = lax.broadcasted_iota(jnp.int32, (count, count), 1)
    return jnp.sum(jnp.where(down == across, column, 0.0), axis=0, keepdims=True)


def dot(left, right):
    return jnp.dot(left, right, preferred_element_type=f32)


def dot_nt(left, right):
    return lax.dot_general(left, right, (((1,), (1,)), ((), ())), preferred_element_type=f32)


def pack_kernel(sizes, *refs):
    far = refs[:4]
    tiles_ref = refs[4]
    near_refs = refs[5:9]
    arrivals = refs[9]
    copies = [pltpu.make_async_copy(a, b, arrivals.at[i]) for i, (a, b) in enumerate(zip(far, near_refs))]
    for copy in copies:
        copy.start()
    for copy in copies:
        copy.wait()
    send_ref, irreps_ref, places_ref, cotangent_ref = near_refs
    _, atoms, width = irreps_ref.shape
    offered = send_ref.shape[0]
    tiles_ref[0] = irreps_ref[0]
    cotangent = cotangent_ref[...]
    tiles_ref[1] = leading(cotangent)
    tiles_ref[2] = trailing(cotangent)
    lane = lax.broadcasted_iota(jnp.int32, (offered, width), 1)
    packed = jnp.zeros((offered, width), f32)
    for number, axis in enumerate(AXES):
        corner = lax.axis_index(axis).astype(f32)
        place = (places_ref[number] + cell_length * corner) / jnp.float32(cell_length * sizes[number])
        place = standing_row(place)
        high = place.astype(bf16).astype(f32)
        middle = (place - high).astype(bf16).astype(f32)
        low = (place - high) - middle
        for level, part in enumerate((high, middle, low)):
            for half in range(atoms // offered):
                rows = part[half * offered : (half + 1) * offered]
                packed = jnp.where(lane == place_lanes * half + 3 * level + number, rows, packed)
    pick_row = lax.broadcasted_iota(jnp.int32, (offered, atoms), 0)
    pick_column = lax.broadcasted_iota(jnp.int32, (offered, atoms), 1)
    wanted = jnp.zeros((offered, atoms), jnp.int32)
    for position in range(offered):
        wanted = jnp.where(pick_row == position, send_ref[position], wanted)
    pick = jnp.where(wanted == pick_column, 1.0, 0.0).astype(bf16)
    rows = dot(pick, jnp.concatenate([irreps_ref[slot] for slot in slots], axis=1))
    pieces = [rows[:, number * width : (number + 1) * width] for number in range(len(slots))]
    tiles_ref[3] = jnp.concatenate([packed, pieces[-1]], axis=0).astype(bf16)
    for pair in range(slot_tiles):
        tiles_ref[atom_tiles + pair] = jnp.concatenate(pieces[2 * pair : 2 * pair + 2], axis=0).astype(bf16)


def prepare_kernel(
    pieces, offered, neighbour_ref, displacement_ref, triples_ref, far_filter_ref, weights_ref, waves_ref, filter_ref, arrival
):
    waves = filter_ref.shape[0]
    shares = far_filter_ref.shape[0] // waves
    first_wave = pl.multiple_of((lax.axis_index("gy") % shares) * waves, waves)
    filter_copy = pltpu.make_async_copy(far_filter_ref.at[pl.ds(first_wave, waves), :], filter_ref, arrival)
    filter_copy.start()
    atoms, count = neighbour_ref.shape
    edges = atoms * count
    depth = weights_ref.shape[1]
    width = waves_ref.shape[1]
    first = displacement_ref[0]
    second = displacement_ref[1]
    third = displacement_ref[2]
    planar = first * first + second * second
    radial = jnp.exp(-(planar + third * third) / radial_width) / math.sqrt(count)
    turn = planar / (planar + planar_floor)
    slot = lax.broadcasted_iota(jnp.int32, (count, edges), 0)
    edge = lax.broadcasted_iota(jnp.int32, (count, edges), 1)
    repeat = jnp.where(edge % count == slot, 1.0, 0.0)
    spread = jnp.dot(
        neighbour_ref[...].astype(f32), repeat, precision=lax.Precision.HIGHEST, preferred_element_type=f32
    )
    owner = lax.broadcasted_iota(jnp.int32, (atoms, edges), 0)
    mine = owner == lax.broadcasted_iota(jnp.int32, (atoms, edges), 1) // count
    index = jnp.sum(jnp.where(mine, spread, 0.0), axis=0, keepdims=True).astype(jnp.int32)
    group = (index - atoms) // offered
    place = (index - atoms) - offered * group
    shift_x = (group >= 9).astype(jnp.int32) + (group >= 18).astype(jnp.int32)
    group = group - 9 * shift_x
    shift_y = (group >= 3).astype(jnp.int32) + (group >= 6).astype(jnp.int32)
    shift_z = group - 3 * shift_y
    line = jnp.zeros_like(index)
    for axis, shift, reach in reversed(tuple(zip(AXES, (shift_x, shift_y, shift_z), pieces))):
        if reach == 2:
            piece = jnp.where(shift == 1, 0, 1)
        else:
            odd = lax.axis_index(axis) % 2
            piece = jnp.where(shift == 1, 0, jnp.where(shift == 2, 1 + odd, 2 - odd))
        line = line * reach + piece
    rows = jnp.where(index < atoms, index, atoms + offered * line + place)
    hits = jnp.where(rows == lax.broadcasted_iota(jnp.int32, (depth, edges), 0), 1.0, 0.0).astype(bf16)
    strengths = [jnp.where(mine, strength, 0.0) for strength in (radial, radial * turn, radial * turn * turn)]
    strengths = jnp.concatenate(strengths, axis=0)
    both = dot_nt(jnp.concatenate([leading(strengths), trailing(strengths)], axis=0), hits)
    total = both[: len(groups) * atoms] + both[len(groups) * atoms :]
    for order in range(len(groups)):
        part = total[order * atoms : (order + 1) * atoms]
        weights_ref[2 * order * atoms : 2 * (order + 1) * atoms, :] = jnp.concatenate(
            [leading(part), trailing(part)], axis=0
        )
    triples = triples_ref[:, pl.ds(first_wave, waves)].astype(f32)
    triples = jnp.concatenate([triples, jnp.zeros((5, triples.shape[1]), f32)], axis=0)
    component = lax.broadcasted_iota(jnp.int32, (8, width), 0)
    lane = lax.broadcasted_iota(jnp.int32, (8, width), 1)
    part = lane % place_lanes
    chosen = jnp.where((part % 3 == component) & (part < 9) & (lane < 2 * place_lanes), 1.0, 0.0)
    waves_ref[...] = lax.dot_general(
        triples.astype(bf16), chosen.astype(bf16), (((0,), (0,)), ((), ())), preferred_element_type=f32
    ).astype(bf16)
    filter_copy.wait()


def ewald_kernel(atom_spots, recipients, shares, wave_step, *refs):
    count_in = 1 + max(spot[0] for spot in atom_spots)
    arrived = refs[:count_in]
    waves_ref, filter_ref = refs[count_in : count_in + 2]
    part_refs = refs[count_in + 2 : count_in + 2 + shares]
    raw_ref, lead_ref, trail_ref, spot_ref, product_ref = refs[count_in + 2 + shares :]
    atoms, width = arrived[0].shape[1:]
    waves = filter_ref.shape[0]
    total_atoms = raw_ref.shape[0]

    upper = lax.broadcasted_iota(jnp.int32, (atoms // 2, width), 1) < place_lanes
    where = 0
    for source, first, blocks in atom_spots:
        ref = arrived[source]

        def place_block(ref, start, row):
            rows = pl.ds(row, atoms)
            raw_ref[rows, :] = ref[start]
            lead_ref[rows, width:] = ref[start + 1]
            trail_ref[rows, width:] = ref[start + 2]
            places = ref[start + 3].astype(f32)[: atoms // 2]
            spot_ref[rows, :] = jnp.concatenate(
                [jnp.where(upper, places, 0.0), jnp.where(upper, 0.0, places)], axis=0
            ).astype(bf16)

        if blocks <= 32:
            for block in range(blocks):
                place_block(ref, first + block * atom_tiles, where + block * atoms)
        else:

            def place_many(block, carry, ref=ref, first=first, where=where):
                place_block(ref, first + block * atom_tiles, pl.multiple_of(where + block * atoms, atoms))
                return carry

            lax.fori_loop(0, blocks, place_many, 0)
        where += blocks * atoms
    charges = raw_ref[...].astype(f32)
    mean = jnp.sum(charges, axis=0, keepdims=True) / total_atoms
    centered = charges - mean
    lead_ref[:, :width] = leading(centered)
    trail_ref[:, :width] = trailing(centered)

    def wave_rows(step):
        return slice(step * wave_step, (step + 1) * wave_step)

    chunk = min(total_atoms, 512)
    mean_total = jnp.zeros((1, width), f32)
    for step in range(waves // wave_step):

        def add_chunk(part, carry):
            factors, plane = carry
            rows = pl.ds(part * chunk, chunk) if isinstance(part, int) else pl.ds(pl.multiple_of(part * chunk, chunk), chunk)
            turns = dot_nt(waves_ref[wave_rows(step), :], spot_ref[rows, :])
            cosine, sine = cos_sin_turns(turns)
            both = jnp.concatenate([cosine, sine], axis=0)
            high = leading(both)
            low = trailing(both)
            factors = factors + (
                dot(high, lead_ref[rows, :]) + dot(high, trail_ref[rows, :]) + dot(low, lead_ref[rows, :])
            )
            return factors, plane + jnp.sum(both, axis=1, keepdims=True)

        start = (jnp.zeros((2 * wave_step, 2 * width), f32), jnp.zeros((2 * wave_step, 1), f32))
        if total_atoms == chunk:
            factors, plane = add_chunk(0, start)
        else:
            factors, plane = lax.fori_loop(0, total_atoms // chunk, add_chunk, start)
        strength = filter_ref[wave_rows(step), :]
        strength = jnp.concatenate([strength, strength], axis=0)
        strength = jnp.concatenate([strength, strength], axis=1)
        product = strength * factors
        mean_total = mean_total + jnp.sum(plane * product[:, width:], axis=0, keepdims=True)
        product_ref[0, step] = leading(product)
        product_ref[1, step] = trailing(product)

    def of_recipients(ref):
        return jnp.concatenate([ref[row : row + atoms, :] for row in recipients], axis=0)

    count = shares * atoms
    spots = of_recipients(spot_ref)
    swapped = []
    for ref in (lead_ref, trail_ref):
        pair = of_recipients(ref)
        swapped.append(jnp.concatenate([pair[:, width:], pair[:, :width]], axis=1))
    pair = jnp.concatenate(swapped, axis=0)
    terms = jnp.zeros((count, 2 * width), f32)
    pushed = jnp.zeros((2 * count, width), f32)
    for step in range(waves // wave_step):
        cosine, sine = cos_sin_turns(dot_nt(spots, waves_ref[wave_rows(step), :]))
        tables = jnp.concatenate([cosine, sine], axis=1)
        tables = jnp.concatenate([leading(tables), trailing(tables)], axis=0)
        high = product_ref[0, step]
        low = product_ref[1, step]
        both = dot(tables, high)
        terms = terms + both[:count] + both[count:] + dot(tables[:count], low)
        both = dot_nt(pair, high)
        against = both[:count] + both[count:] + dot_nt(pair[:count], low)
        slope = cosine * against[:, wave_step:] - sine * against[:, :wave_step]
        slope = jnp.concatenate([leading(slope), trailing(slope)], axis=0)
        pushed = pushed + dot(slope, waves_ref[wave_rows(step), :])
    charge = terms[:, width:] - mean_total / total_atoms
    pushed = pushed[:count] + pushed[count:]
    for number, ref in enumerate(part_refs):
        rows = slice(number * atoms, (number + 1) * atoms)
        ref[0] = terms[rows, :width]
        ref[1] = charge[rows]
        ref[2] = pushed[rows]


def edge_kernel(sizes, scale, halo_spots, part_count, *refs):
    count_in = len(refs) - part_count - 10
    arrived = refs[:count_in]
    part_refs = refs[count_in : count_in + part_count]
    irreps_ref, weights_ref, zero_ref, one_ref, two_ref = refs[count_in + part_count : count_in + part_count + 5]
    updated_ref, long_ref, charge_ref, place_ref, table_ref = refs[count_in + part_count + 5 :]
    harmonics, atoms, width = irreps_ref.shape
    offered = atoms // 2

    sums = []
    for number in range(3):
        total = part_refs[0][number]
        for ref in part_refs[1:]:
            total = total + ref[number]
        sums.append(scale * total)
    long_ref[...] = sums[0]
    charge_ref[...] = sums[1]
    for number, size in enumerate(sizes):
        factor = 2.0 * math.pi / (cell_length * size)
        place_ref[number] = factor * lying_column(sums[2][:, number : number + 1])

    used = atoms + offered * len(halo_spots)
    if len(halo_spots) % 2:
        used -= offered
    table_ref[used:, :] = jnp.zeros((table_ref.shape[0] - used, table_ref.shape[1]), bf16)
    for number, slot in enumerate(slots):
        table_ref[:atoms, number * width : (number + 1) * width] = irreps_ref[slot]

    def put(first, number, pieces):
        if len(pieces) == 1:
            pieces = pieces + [jnp.zeros((offered, width), f32)]
        table_ref[
            atoms + first * offered : atoms + (first + 2) * offered, number * width : (number + 1) * width
        ] = jnp.concatenate(pieces, axis=0).astype(bf16)

    for first in range(0, len(halo_spots), 2):
        spots = halo_spots[first : first + 2]
        for tile in range(slot_tiles):
            wide = [arrived[source][start + tile].astype(f32) for source, start, _, _ in spots]
            put(first, 2 * tile, [piece[:offered] for piece in wide])
            put(first, 2 * tile + 1, [piece[offered:] for piece in wide])
        wide = [arrived[source][tile].astype(f32) for _, _, source, tile in spots]
        put(first, len(slots) - 1, [piece[offered:] for piece in wide])
    outputs = {}
    lane = 0
    for order, (group, mixing_ref) in enumerate(zip(groups, (zero_ref, one_ref, two_ref))):
        span = len(group) * width
        both = dot(weights_ref[2 * order * atoms : 2 * (order + 1) * atoms, :], table_ref[:, lane : lane + span])
        lane += span
        gathered = both[:atoms] + both[atoms:]
        if order == 0:
            both = dot(jnp.concatenate([leading(gathered), trailing(gathered)], axis=0), mixing_ref[...])
            mixed = both[:atoms] + both[atoms:]
        else:
            half = span // 2
            plus, minus = gathered[:, :half], gathered[:, half:]
            both = dot(
                jnp.concatenate([leading(plus), leading(minus), trailing(plus), trailing(minus)], axis=0),
                mixing_ref[...],
            )
            both = both[: 2 * atoms] + both[2 * atoms :]
            mixed = jnp.concatenate(
                [both[:atoms, :half] - both[atoms:, half:], both[atoms:, :half] + both[:atoms, half:]], axis=1
            )
        for number, slot in enumerate(group):
            outputs[slot] = mixed[:, number * width : (number + 1) * width]
    for slot in range(harmonics):
        if slot in outputs:
            updated_ref[slot] = (irreps_ref[slot].astype(f32) + outputs[slot]).astype(bf16)
        else:
            updated_ref[slot] = irreps_ref[slot]


def swap(value, sizes, partner):
    perm = []
    for x in range(sizes[0]):
        for y in range(sizes[1]):
            for z in range(sizes[2]):
                a, b, c = partner(x, y, z)
                perm.append(((x * sizes[1] + y) * sizes[2] + z, (a * sizes[1] + b) * sizes[2] + c))
    return lax.ppermute(value, AXES, perm)


def pair_of(index, size):
    return index ^ 1


def other_of(index, size):
    return (index - 1) % size if index % 2 == 0 else (index + 1) % size


def exchange(tiles, sizes):
    size_x, size_y, size_z = sizes
    if size_x == 4 and size_y == 4 and size_z == 2:
        paired = swap(tiles, sizes, lambda x, y, z: (x ^ 1, y, z))
        across = swap(tiles, sizes, lambda x, y, z: (x ^ 3, y, z))
        skipped = swap(tiles[:atom_tiles], sizes, lambda x, y, z: (x ^ 2, y, z))
        atoms = jnp.concatenate([tiles[:atom_tiles], paired[:atom_tiles], skipped, across[:atom_tiles]])
        halo = jnp.concatenate([tiles[atom_tiles:], paired[atom_tiles:], across[atom_tiles:]])

        def by_y(x, y, z):
            return (x, y ^ 3, z)

        def by_z(x, y, z):
            return (x, y, z ^ 1)

        def by_both(x, y, z):
            return (x, y ^ 3, z ^ 1)

        def by_core(x, y, z):
            return (x, y ^ 1, z)

        far = [swap(atoms, sizes, by_y), swap(atoms, sizes, by_z)]
        far = jnp.concatenate(far + [swap(atoms, sizes, by_both)])
        atom_arrays = [atoms, far, swap(atoms, sizes, by_core), swap(far, sizes, by_core)]
        halo_y = swap(halo, sizes, by_y)
        halo_z = swap(halo, sizes, by_z)
        halo_both = swap(halo, sizes, by_both)
        halo_core = swap(halo, sizes, by_core)
        halo_z_core = swap(halo_z, sizes, by_core)
        halo_arrays = [halo, halo_core, halo_y, halo_z, halo_z_core, halo_both]
        atom_spots = [(number, 0, array.shape[0] // atom_tiles) for number, array in enumerate(atom_arrays)]
        beside = ((0, 0), (2, 0), (1, 0), (1, 4 * atom_tiles), (3, 4 * atom_tiles), (1, 8 * atom_tiles))
        halo_spots = [
            (number, slot_tiles * piece, len(halo_arrays) + source, first + atom_tiles * block + atom_tiles - 1)
            for number, (source, first) in enumerate(beside)
            for piece, block in enumerate((0, 1, 3))
        ]
        total_rows = sum(spot[2] for spot in atom_spots) * tiles.shape[1]
        return atom_arrays, atom_spots, halo_arrays + atom_arrays, halo_spots, (0, total_rows // 2)
    everyone = lax.all_gather(tiles[:atom_tiles], AXES, axis=0, tiled=True)
    everyone = jnp.roll(everyone, -lax.axis_index(AXES) * atom_tiles, axis=0)
    layers = [tiles[atom_tiles - 1 :]]
    for number in range(3):
        arrived = []
        for partner in (pair_of, other_of)[: 1 if sizes[number] == 2 else 2]:

            def step(*place, number=number, partner=partner):
                place = list(place)
                place[number] = partner(place[number], sizes[number])
                return place

            arrived += [swap(part, sizes, step) for part in layers]
        layers = layers + arrived
    return [everyone], [(0, 0, math.prod(sizes))], layers, [(number, 1, number, 0) for number in range(len(layers))], (0,)


def vmem():
    return pl.BlockSpec(memory_space=pltpu.VMEM)


def far():
    return pl.BlockSpec(memory_space=pltpu.HBM)


def grant(mebibytes):
    return pltpu.CompilerParams(vmem_limit_bytes=mebibytes * 2**20)


def stay(value):
    return pltpu.with_memory_space_constraint(value, pltpu.HBM)


def near(value):
    return pltpu.with_memory_space_constraint(value, pltpu.VMEM)


def layer(
    node_irreps,
    positions,
    send_list,
    neighbours,
    displacements,
    order_zero,
    order_one,
    order_two,
    reciprocal_triples,
    reciprocal_filter,
    cotangent,
):
    sizes = tuple(lax.axis_size(axis) for axis in AXES)
    irreps = jnp.transpose(node_irreps[0, 0, 0], (1, 0, 2))
    harmonics, atoms, width = irreps.shape
    sent = send_list[0, 0, 0]
    offered = sent.shape[0]
    neighbour = neighbours[0, 0, 0]
    waves = reciprocal_filter.shape[0]
    total_atoms = atoms * math.prod(sizes)
    own_cotangent = cotangent[0, 0, 0]

    tiles = pl.pallas_call(
        functools.partial(pack_kernel, sizes),
        out_shape=jax.ShapeDtypeStruct((atom_tiles + slot_tiles, atoms, width), bf16),
        in_specs=[far() for _ in range(4)],
        out_specs=vmem(),
        scratch_shapes=[
            pltpu.SMEM(sent.shape, jnp.int32),
            pltpu.VMEM(irreps.shape, bf16),
            pltpu.VMEM((3, 1, atoms), f32),
            pltpu.VMEM(own_cotangent.shape, f32),
            pltpu.SemaphoreType.DMA((4,)),
        ],
        compiler_params=grant(4),
        name="pack",
    )(*map(stay, (sent, irreps, positions[0, 0, 0][:, None, :], own_cotangent)))

    atom_arrays, atom_spots, halo_arrays, halo_spots, recipients = exchange(tiles, sizes)
    shares = len(recipients)
    pieces = tuple(2 if size == 2 else 3 for size in sizes)
    depth = -(-(atoms + offered * math.prod(pieces)) // 256) * 256

    weights, spread, strengths = pl.pallas_call(
        functools.partial(prepare_kernel, pieces, offered),
        out_shape=(
            jax.ShapeDtypeStruct((2 * len(groups) * atoms, depth), bf16),
            jax.ShapeDtypeStruct((waves // shares, width), bf16),
            jax.ShapeDtypeStruct((waves // shares, width), f32),
        ),
        in_specs=[vmem(), vmem(), vmem(), far()],
        out_specs=(vmem(), vmem(), vmem()),
        scratch_shapes=[pltpu.SemaphoreType.DMA],
        compiler_params=grant(6),
        name="prepare",
    )(
        *map(near, (neighbour, displacements[0, 0, 0][:, None, :], reciprocal_triples.T)), stay(reciprocal_filter)
    )

    wave_step = 128
    part_shape = jax.ShapeDtypeStruct((3, atoms, width), f32)
    parts = pl.pallas_call(
        functools.partial(ewald_kernel, tuple(atom_spots), recipients, shares, wave_step),
        out_shape=[part_shape] * shares,
        in_specs=[vmem() for _ in range(len(atom_arrays) + 2)],
        out_specs=[vmem()] * shares,
        scratch_shapes=[
            pltpu.VMEM((total_atoms, width), bf16),
            pltpu.VMEM((total_atoms, 2 * width), bf16),
            pltpu.VMEM((total_atoms, 2 * width), bf16),
            pltpu.VMEM((total_atoms, width), bf16),
            pltpu.VMEM((2, waves // shares // wave_step, 2 * wave_step, 2 * width), bf16),
        ],
        compiler_params=grant(12 + total_atoms // 256),
        name="ewald",
    )(*map(near, (*atom_arrays, spread, strengths)))
    parts = list(parts)
    if shares > 1:
        parts[1] = swap(parts[1], sizes, lambda x, y, z: (x, y ^ 1, z))

    scale = 1.0 / math.sqrt(total_atoms * waves)
    updated, long_range, charge_grad, position_grad = pl.pallas_call(
        functools.partial(edge_kernel, sizes, scale, tuple(halo_spots), shares),
        out_shape=(
            jax.ShapeDtypeStruct((harmonics, atoms, width), bf16),
            jax.ShapeDtypeStruct((atoms, width), f32),
            jax.ShapeDtypeStruct((atoms, width), f32),
            jax.ShapeDtypeStruct((3, 1, atoms), f32),
        ),
        in_specs=[vmem() for _ in range(len(halo_arrays) + shares + 5)],
        out_specs=tuple(vmem() for _ in range(4)),
        scratch_shapes=[pltpu.VMEM((depth, len(slots) * width), bf16)],
        compiler_params=grant(12),
        name="edges",
    )(*map(near, (*halo_arrays, *parts, irreps, weights, order_zero, order_one, order_two)))
    outs = (jnp.transpose(updated, (1, 0, 2)), long_range, charge_grad, position_grad[:, 0, :])
    return tuple(out[None, None, None] for out in outs)


def solution(mesh):
    return jax.shard_map(
        layer,
        mesh=mesh,
        in_specs=(
            P("gx", "gy", "gz", None, None, None),
            P("gx", "gy", "gz", None, None),
            P("gx", "gy", "gz", None),
            P("gx", "gy", "gz", None, None),
            P("gx", "gy", "gz", None, None),
            P(),
            P(),
            P(),
            P(),
            P(),
            P("gx", "gy", "gz", None, None),
        ),
        out_specs=(
            P("gx", "gy", "gz", None, None, None),
            P("gx", "gy", "gz", None, None),
            P("gx", "gy", "gz", None, None),
            P("gx", "gy", "gz", None, None),
        ),
        check_vma=False,
    )
```

```python
import functools
import math

import jax
import jax.numpy as jnp
from jax import lax
from jax.experimental import pallas as pl
from jax.experimental.pallas import tpu as pltpu
from jax.sharding import PartitionSpec as P


AXES = ("gx", "gy", "gz")
cell_length = 6.8
planar_floor = 0.25
radial_width = 64.0
top_degree = 4
top_order = 2
bf16 = jnp.bfloat16
f32 = jnp.float32


def slot_of(degree, order):
    return degree * degree + degree + order


groups = [[slot_of(l, 0) for l in range(top_degree + 1)]]
for order in range(1, top_order + 1):
    groups.append([slot_of(l, sign * order) for sign in (1, -1) for l in range(order, top_degree + 1)])
slots = [slot for group in groups for slot in group]
slot_tiles = len(slots) // 2
atom_tiles = 4
place_lanes = 16


def leading(values):
    return values.astype(bf16)


def trailing(values):
    return (values - values.astype(bf16).astype(f32)).astype(bf16)


def cos_sin_turns(turns):
    rest = turns - ((turns + whole_bias) - whole_bias)
    square = rest * rest
    half_cosine = jnp.full_like(square, cos_series[-1])
    for factor in cos_series[-2::-1]:
        half_cosine = half_cosine * square + factor
    half_sine = jnp.full_like(square, sin_series[-1])
    for factor in sin_series[-2::-1]:
        half_sine = half_sine * square + factor
    half_sine = half_sine * rest
    return 1.0 - half_sine * half_sine, half_cosine * half_sine


whole_bias = 1.5 * 2.0**23


def fitted(function, count):
    import numpy as np

    nodes = np.cos((np.arange(count) + 0.5) * np.pi / count)
    line = np.polynomial.chebyshev.chebfit(nodes, function((nodes + 1.0) / 8.0), count - 1)
    power = np.polynomial.chebyshev.cheb2poly(line)
    shift = np.polynomial.polynomial.Polynomial([-1.0, 8.0])
    total = np.polynomial.polynomial.Polynomial([0.0])
    for factor in power[::-1]:
        total = total * shift + factor
    return [float(factor) for factor in total.coef]


def _cos_of(s):
    import numpy as np

    return np.sqrt(2.0) * np.cos(np.pi * np.sqrt(s))


def _sin_of(s):
    import numpy as np

    return np.sqrt(2.0) * np.sin(np.pi * np.sqrt(s)) / np.sqrt(s)


cos_series = fitted(_cos_of, 6)
sin_series = fitted(_sin_of, 5)


def standing_row(row):
    count = row.shape[1]
    down = lax.broadcasted_iota(jnp.int32, (count, count), 0)
    across = lax.broadcasted_iota(jnp.int32, (count, count), 1)
    return jnp.sum(jnp.where(down == across, row, 0.0), axis=1, keepdims=True)


def lying_column(column):
    count = column.shape[0]
    down = lax.broadcasted_iota(jnp.int32, (count, count), 0)
    across = lax.broadcasted_iota(jnp.int32, (count, count), 1)
    return jnp.sum(jnp.where(down == across, column, 0.0), axis=0, keepdims=True)


def dot(left, right):
    return jnp.dot(left, right, preferred_element_type=f32)


def dot_nt(left, right):
    return lax.dot_general(left, right, (((1,), (1,)), ((), ())), preferred_element_type=f32)


def pack_kernel(sizes, *refs):
    far = refs[:4]
    tiles_ref, atoms_ref = refs[4:6]
    near_refs = refs[6:10]
    arrivals = refs[10]
    copies = [pltpu.make_async_copy(a, b, arrivals.at[i]) for i, (a, b) in enumerate(zip(far, near_refs))]
    for copy in copies:
        copy.start()
    for copy in copies:
        copy.wait()
    send_ref, irreps_ref, places_ref, cotangent_ref = near_refs
    _, atoms, width = irreps_ref.shape
    offered = send_ref.shape[0]
    tiles_ref[0] = irreps_ref[0]
    cotangent = cotangent_ref[...]
    tiles_ref[1] = leading(cotangent)
    tiles_ref[2] = trailing(cotangent)
    lane = lax.broadcasted_iota(jnp.int32, (offered, width), 1)
    packed = jnp.zeros((offered, width), f32)
    for number, axis in enumerate(AXES):
        corner = lax.axis_index(axis).astype(f32)
        place = (places_ref[number] + cell_length * corner) / jnp.float32(cell_length * sizes[number])
        place = standing_row(place)
        high = place.astype(bf16).astype(f32)
        middle = (place - high).astype(bf16).astype(f32)
        low = (place - high) - middle
        for level, part in enumerate((high, middle, low)):
            for half in range(atoms // offered):
                rows = part[half * offered : (half + 1) * offered]
                packed = jnp.where(lane == place_lanes * half + 3 * level + number, rows, packed)
    pick_row = lax.broadcasted_iota(jnp.int32, (offered, atoms), 0)
    pick_column = lax.broadcasted_iota(jnp.int32, (offered, atoms), 1)
    wanted = jnp.zeros((offered, atoms), jnp.int32)
    for position in range(offered):
        wanted = jnp.where(pick_row == position, send_ref[position], wanted)
    pick = jnp.where(wanted == pick_column, 1.0, 0.0).astype(bf16)
    rows = dot(pick, jnp.concatenate([irreps_ref[slot] for slot in slots], axis=1))
    pieces = [rows[:, number * width : (number + 1) * width] for number in range(len(slots))]
    tiles_ref[3] = jnp.concatenate([packed, pieces[-1]], axis=0).astype(bf16)
    for pair in range(slot_tiles):
        tiles_ref[atom_tiles + pair] = jnp.concatenate(pieces[2 * pair : 2 * pair + 2], axis=0).astype(bf16)
    atoms_ref[...] = tiles_ref[:atom_tiles]


def join_kernel(own_ref, paired_ref, skipped_ref, across_ref, atoms_ref, halo_ref):
    for number, ref in enumerate((own_ref, paired_ref, skipped_ref, across_ref)):
        atoms_ref[number * atom_tiles : (number + 1) * atom_tiles] = ref[:atom_tiles]
    for number, ref in enumerate((own_ref, paired_ref, across_ref)):
        halo_ref[number * slot_tiles : (number + 1) * slot_tiles] = ref[atom_tiles:]


def prepare_kernel(
    pieces, offered, neighbour_ref, displacement_ref, triples_ref, far_filter_ref, weights_ref, waves_ref, filter_ref, arrival
):
    waves = filter_ref.shape[0]
    shares = far_filter_ref.shape[0] // waves
    first_wave = pl.multiple_of((lax.axis_index("gy") % shares) * waves, waves)
    filter_copy = pltpu.make_async_copy(far_filter_ref.at[pl.ds(first_wave, waves), :], filter_ref, arrival)
    filter_copy.start()
    atoms, count = neighbour_ref.shape
    edges = atoms * count
    depth = weights_ref.shape[1]
    width = waves_ref.shape[1]
    first = displacement_ref[0]
    second = displacement_ref[1]
    third = displacement_ref[2]
    planar = first * first + second * second
    radial = jnp.exp(-(planar + third * third) / radial_width) / math.sqrt(count)
    turn = planar / (planar + planar_floor)
    slot = lax.broadcasted_iota(jnp.int32, (count, edges), 0)
    edge = lax.broadcasted_iota(jnp.int32, (count, edges), 1)
    repeat = jnp.where(edge % count == slot, 1.0, 0.0)
    spread = jnp.dot(
        neighbour_ref[...].astype(f32), repeat, precision=lax.Precision.HIGHEST, preferred_element_type=f32
    )
    owner = lax.broadcasted_iota(jnp.int32, (atoms, edges), 0)
    mine = owner == lax.broadcasted_iota(jnp.int32, (atoms, edges), 1) // count
    index = jnp.sum(jnp.where(mine, spread, 0.0), axis=0, keepdims=True).astype(jnp.int32)
    group = (index - atoms) // offered
    place = (index - atoms) - offered * group
    shift_x = (group >= 9).astype(jnp.int32) + (group >= 18).astype(jnp.int32)
    group = group - 9 * shift_x
    shift_y = (group >= 3).astype(jnp.int32) + (group >= 6).astype(jnp.int32)
    shift_z = group - 3 * shift_y
    line = jnp.zeros_like(index)
    for axis, shift, reach in reversed(tuple(zip(AXES, (shift_x, shift_y, shift_z), pieces))):
        if reach == 2:
            piece = jnp.where(shift == 1, 0, 1)
        else:
            odd = lax.axis_index(axis) % 2
            piece = jnp.where(shift == 1, 0, jnp.where(shift == 2, 1 + odd, 2 - odd))
        line = line * reach + piece
    rows = jnp.where(index < atoms, index, atoms + offered * line + place)
    hits = jnp.where(rows == lax.broadcasted_iota(jnp.int32, (depth, edges), 0), 1.0, 0.0).astype(bf16)
    strengths = [jnp.where(mine, strength, 0.0) for strength in (radial, radial * turn, radial * turn * turn)]
    strengths = jnp.concatenate(strengths, axis=0)
    both = dot_nt(jnp.concatenate([leading(strengths), trailing(strengths)], axis=0), hits)
    total = both[: len(groups) * atoms] + both[len(groups) * atoms :]
    for order in range(len(groups)):
        part = total[order * atoms : (order + 1) * atoms]
        weights_ref[2 * order * atoms : 2 * (order + 1) * atoms, :] = jnp.concatenate(
            [leading(part), trailing(part)], axis=0
        )
    triples = triples_ref[:, pl.ds(first_wave, waves)].astype(f32)
    triples = jnp.concatenate([triples, jnp.zeros((5, triples.shape[1]), f32)], axis=0)
    component = lax.broadcasted_iota(jnp.int32, (8, width), 0)
    lane = lax.broadcasted_iota(jnp.int32, (8, width), 1)
    part = lane % place_lanes
    chosen = jnp.where((part % 3 == component) & (part < 9) & (lane < 2 * place_lanes), 1.0, 0.0)
    waves_ref[...] = lax.dot_general(
        triples.astype(bf16), chosen.astype(bf16), (((0,), (0,)), ((), ())), preferred_element_type=f32
    ).astype(bf16)
    filter_copy.wait()


def lay_out(arrived, atom_spots, lead_ref, trail_ref, spot_ref):
    atoms, width = arrived[0].shape[1:]
    upper = lax.broadcasted_iota(jnp.int32, (atoms // 2, width), 1) < place_lanes
    where = 0
    for source, first, blocks in atom_spots:
        ref = arrived[source]

        def place_block(ref, start, row):
            rows = pl.ds(row, atoms)
            lead_ref[rows, :width] = ref[start]
            lead_ref[rows, width:] = ref[start + 1]
            trail_ref[rows, :] = ref[start + 2]
            places = ref[start + 3].astype(f32)[: atoms // 2]
            spot_ref[rows, :] = jnp.concatenate(
                [jnp.where(upper, places, 0.0), jnp.where(upper, 0.0, places)], axis=0
            ).astype(bf16)

        if blocks <= 32:
            for block in range(blocks):
                place_block(ref, first + block * atom_tiles, where + block * atoms)
        else:

            def place_many(block, carry, ref=ref, first=first, where=where):
                place_block(ref, first + block * atom_tiles, pl.multiple_of(where + block * atoms, atoms))
                return carry

            lax.fori_loop(0, blocks, place_many, 0)
        where += blocks * atoms


def wave_sums(waves, lead_ref, trail_ref, spot_ref):
    total = lead_ref.shape[0]
    width = trail_ref.shape[1]
    chunk = min(total, 512)

    def add_chunk(part, carry):
        charge_sums, response_sums, plane = carry
        rows = pl.ds(part * chunk, chunk) if isinstance(part, int) else pl.ds(pl.multiple_of(part * chunk, chunk), chunk)
        cosine, sine = cos_sin_turns(dot_nt(waves, spot_ref[rows, :]))
        both = jnp.concatenate([cosine, sine], axis=0)
        high = leading(both)
        low = trailing(both)
        main = dot(high, lead_ref[rows, :]) + dot(low, lead_ref[rows, :])
        return (
            charge_sums + main[:, :width],
            response_sums + (main[:, width:] + dot(high, trail_ref[rows, :])),
            plane + jnp.sum(both, axis=1, keepdims=True),
        )

    lines = 2 * waves.shape[0]
    carry = (jnp.zeros((lines, width), f32), jnp.zeros((lines, width), f32), jnp.zeros((lines, 1), f32))
    if total == chunk:
        return add_chunk(0, carry)
    return lax.fori_loop(0, total // chunk, add_chunk, carry)


def factor_kernel(atom_spots, wave_step, count_in, *refs):
    arrived = refs[:count_in]
    waves_ref, sums_ref, plane_ref, charge_ref, lead_ref, trail_ref, spot_ref = refs[count_in:]
    width = trail_ref.shape[1]
    lay_out(arrived, atom_spots, lead_ref, trail_ref, spot_ref)
    charge_ref[...] = jnp.sum(lead_ref[:, :width].astype(f32), axis=0, keepdims=True)
    for step in range(waves_ref.shape[0] // wave_step):
        sums = wave_sums(waves_ref[step * wave_step : (step + 1) * wave_step, :], lead_ref, trail_ref, spot_ref)
        sums_ref[step, :, :width] = sums[0]
        sums_ref[step, :, width:] = sums[1]
        plane_ref[step] = sums[2]


def ewald_kernel(atom_spots, wave_step, total_atoms, shares, count_in, *refs):
    arrived = refs[:count_in]
    own_ref, waves_ref, filter_ref, sums_ref, plane_ref, charge_ref = refs[count_in : count_in + 6]
    part_refs = refs[count_in + 6 : count_in + 6 + shares]
    product_ref = refs[count_in + 6 + shares]
    laid = refs[count_in + 7 + shares :]
    atoms, width = own_ref.shape[1:]
    waves = filter_ref.shape[0]
    mean = charge_ref[...]
    if atom_spots:
        lay_out(arrived, atom_spots, *laid)
        mean = mean + jnp.sum(laid[0][:, :width].astype(f32), axis=0, keepdims=True)
    mean = mean / total_atoms

    def wave_rows(step):
        return slice(step * wave_step, (step + 1) * wave_step)

    mean_total = jnp.zeros((1, width), f32)
    for step in range(waves // wave_step):
        charge_sums = sums_ref[step, :, :width]
        response_sums = sums_ref[step, :, width:]
        plane = plane_ref[step]
        if atom_spots:
            more = wave_sums(waves_ref[wave_rows(step), :], *laid)
            charge_sums = charge_sums + more[0]
            response_sums = response_sums + more[1]
            plane = plane + more[2]
        strength = filter_ref[wave_rows(step), :]
        strength = jnp.concatenate([strength, strength], axis=0)
        product = jnp.concatenate([strength * (charge_sums - plane * mean), strength * response_sums], axis=1)
        mean_total = mean_total + jnp.sum(plane * product[:, width:], axis=0, keepdims=True)
        product_ref[0, step] = leading(product)
        product_ref[1, step] = trailing(product)

    upper = lax.broadcasted_iota(jnp.int32, (atoms // 2, width), 1) < place_lanes
    owners = [own_ref] + ([arrived[0]] if shares > 1 else [])
    count = shares * atoms
    spots = []
    for ref in owners:
        places = ref[3].astype(f32)[: atoms // 2]
        spots += [jnp.where(upper, places, 0.0), jnp.where(upper, 0.0, places)]
    spots = jnp.concatenate(spots, axis=0).astype(bf16)
    centered = jnp.concatenate([ref[0].astype(f32) for ref in owners], axis=0) - mean
    cotangents = [jnp.concatenate([ref[number] for ref in owners], axis=0) for number in (1, 2)]
    pair = jnp.concatenate(
        [
            jnp.concatenate([cotangents[0], leading(centered)], axis=1),
            jnp.concatenate([cotangents[1], trailing(centered)], axis=1),
        ],
        axis=0,
    )
    terms = jnp.zeros((count, 2 * width), f32)
    pushed = jnp.zeros((2 * count, width), f32)
    for step in range(waves // wave_step):
        cosine, sine = cos_sin_turns(dot_nt(spots, waves_ref[wave_rows(step), :]))
        tables = jnp.concatenate([cosine, sine], axis=1)
        tables = jnp.concatenate([leading(tables), trailing(tables)], axis=0)
        high = product_ref[0, step]
        low = product_ref[1, step]
        both = dot(tables, high)
        terms = terms + both[:count] + both[count:] + dot(tables[:count], low)
        both = dot_nt(pair, high)
        against = both[:count] + both[count:] + dot_nt(pair[:count], low)
        slope = cosine * against[:, wave_step:] - sine * against[:, :wave_step]
        slope = jnp.concatenate([leading(slope), trailing(slope)], axis=0)
        pushed = pushed + dot(slope, waves_ref[wave_rows(step), :])
    charge = terms[:, width:] - mean_total / total_atoms
    pushed = pushed[:count] + pushed[count:]
    for number, ref in enumerate(part_refs):
        rows = slice(number * atoms, (number + 1) * atoms)
        ref[0] = terms[rows, :width]
        ref[1] = charge[rows]
        ref[2] = pushed[rows]


def edge_kernel(sizes, scale, halo_spots, part_count, *refs):
    count_in = len(refs) - part_count - 10
    arrived = refs[:count_in]
    part_refs = refs[count_in : count_in + part_count]
    irreps_ref, weights_ref, zero_ref, one_ref, two_ref = refs[count_in + part_count : count_in + part_count + 5]
    updated_ref, long_ref, charge_ref, place_ref, table_ref = refs[count_in + part_count + 5 :]
    harmonics, atoms, width = irreps_ref.shape
    offered = atoms // 2

    sums = []
    for number in range(3):
        total = part_refs[0][number]
        for ref in part_refs[1:]:
            total = total + ref[number]
        sums.append(scale * total)
    long_ref[...] = sums[0]
    charge_ref[...] = sums[1]
    for number, size in enumerate(sizes):
        factor = 2.0 * math.pi / (cell_length * size)
        place_ref[number] = factor * lying_column(sums[2][:, number : number + 1])

    used = atoms + offered * len(halo_spots)
    if len(halo_spots) % 2:
        used -= offered
    table_ref[used:, :] = jnp.zeros((table_ref.shape[0] - used, table_ref.shape[1]), bf16)
    for number, slot in enumerate(slots):
        table_ref[:atoms, number * width : (number + 1) * width] = irreps_ref[slot]

    def put(first, number, pieces):
        if len(pieces) == 1:
            pieces = pieces + [jnp.zeros((offered, width), f32)]
        table_ref[
            atoms + first * offered : atoms + (first + 2) * offered, number * width : (number + 1) * width
        ] = jnp.concatenate(pieces, axis=0).astype(bf16)

    for first in range(0, len(halo_spots), 2):
        spots = halo_spots[first : first + 2]
        for tile in range(slot_tiles):
            wide = [arrived[source][start + tile].astype(f32) for source, start, _, _ in spots]
            put(first, 2 * tile, [piece[:offered] for piece in wide])
            put(first, 2 * tile + 1, [piece[offered:] for piece in wide])
        wide = [arrived[source][tile].astype(f32) for _, _, source, tile in spots]
        put(first, len(slots) - 1, [piece[offered:] for piece in wide])
    outputs = {}
    lane = 0
    for order, (group, mixing_ref) in enumerate(zip(groups, (zero_ref, one_ref, two_ref))):
        span = len(group) * width
        both = dot(weights_ref[2 * order * atoms : 2 * (order + 1) * atoms, :], table_ref[:, lane : lane + span])
        lane += span
        gathered = both[:atoms] + both[atoms:]
        if order == 0:
            both = dot(jnp.concatenate([leading(gathered), trailing(gathered)], axis=0), mixing_ref[...])
            mixed = both[:atoms] + both[atoms:]
        else:
            half = span // 2
            plus, minus = gathered[:, :half], gathered[:, half:]
            both = dot(
                jnp.concatenate([leading(plus), leading(minus), trailing(plus), trailing(minus)], axis=0),
                mixing_ref[...],
            )
            both = both[: 2 * atoms] + both[2 * atoms :]
            mixed = jnp.concatenate(
                [both[:atoms, :half] - both[atoms:, half:], both[atoms:, :half] + both[:atoms, half:]], axis=1
            )
        for number, slot in enumerate(group):
            outputs[slot] = mixed[:, number * width : (number + 1) * width]
    for slot in range(harmonics):
        if slot in outputs:
            updated_ref[slot] = (irreps_ref[slot].astype(f32) + outputs[slot]).astype(bf16)
        else:
            updated_ref[slot] = irreps_ref[slot]


def swap(value, sizes, partner):
    perm = []
    for x in range(sizes[0]):
        for y in range(sizes[1]):
            for z in range(sizes[2]):
                a, b, c = partner(x, y, z)
                perm.append(((x * sizes[1] + y) * sizes[2] + z, (a * sizes[1] + b) * sizes[2] + c))
    return lax.ppermute(value, AXES, perm)


def pair_of(index, size):
    return index ^ 1


def other_of(index, size):
    return (index - 1) % size if index % 2 == 0 else (index + 1) % size


def exchange(tiles, own_atoms, sizes):
    size_x, size_y, size_z = sizes
    if size_x == 4 and size_y == 4 and size_z == 2:
        paired = swap(tiles, sizes, lambda x, y, z: (x ^ 1, y, z))
        across = swap(tiles, sizes, lambda x, y, z: (x ^ 3, y, z))
        skipped = swap(own_atoms, sizes, lambda x, y, z: (x ^ 2, y, z))
        atoms, halo = pl.pallas_call(
            join_kernel,
            out_shape=[
                jax.ShapeDtypeStruct((count,) + tiles.shape[1:], bf16) for count in (4 * atom_tiles, 3 * slot_tiles)
            ],
            in_specs=[vmem() for _ in range(4)],
            out_specs=[vmem() for _ in range(2)],
            compiler_params=grant(2),
            name="join",
        )(*map(near, (tiles, paired, skipped, across)))

        def by_y(x, y, z):
            return (x, y ^ 3, z)

        def by_z(x, y, z):
            return (x, y, z ^ 1)

        def by_both(x, y, z):
            return (x, y ^ 3, z ^ 1)

        def by_core(x, y, z):
            return (x, y ^ 1, z)

        far = [swap(atoms, sizes, by_y), swap(atoms, sizes, by_z)]
        far = jnp.concatenate([atoms] + far + [swap(atoms, sizes, by_both)])
        atom_arrays = [far, swap(far, sizes, by_core)]
        halo_y = swap(halo, sizes, by_y)
        halo_z = swap(halo, sizes, by_z)
        halo_both = swap(halo, sizes, by_both)
        halo_core = swap(halo, sizes, by_core)
        halo_z_core = swap(halo_z, sizes, by_core)
        halo_arrays = [halo, halo_core, halo_y, halo_z, halo_z_core, halo_both]
        atom_spots = [(number, 0, array.shape[0] // atom_tiles) for number, array in enumerate(atom_arrays)]
        line = 4 * atom_tiles
        beside = ((0, 0), (1, 0), (0, line), (0, 2 * line), (1, 2 * line), (0, 3 * line))
        halo_spots = [
            (number, slot_tiles * piece, len(halo_arrays) + source, first + atom_tiles * block + atom_tiles - 1)
            for number, (source, first) in enumerate(beside)
            for piece, block in enumerate((0, 1, 3))
        ]
        return atom_arrays, atom_spots, halo_arrays + atom_arrays, halo_spots, 2
    everyone = lax.all_gather(own_atoms, AXES, axis=0, tiled=True)
    everyone = jnp.roll(everyone, -lax.axis_index(AXES) * atom_tiles, axis=0)
    layers = [tiles[atom_tiles - 1 :]]
    for number in range(3):
        arrived = []
        for partner in (pair_of, other_of)[: 1 if sizes[number] == 2 else 2]:

            def step(*place, number=number, partner=partner):
                place = list(place)
                place[number] = partner(place[number], sizes[number])
                return place

            arrived += [swap(part, sizes, step) for part in layers]
        layers = layers + arrived
    return [everyone], [(0, 0, math.prod(sizes))], layers, [(number, 1, number, 0) for number in range(len(layers))], 1


def vmem():
    return pl.BlockSpec(memory_space=pltpu.VMEM)


def far():
    return pl.BlockSpec(memory_space=pltpu.HBM)


def grant(mebibytes):
    return pltpu.CompilerParams(vmem_limit_bytes=mebibytes * 2**20)


def stay(value):
    return pltpu.with_memory_space_constraint(value, pltpu.HBM)


def near(value):
    return pltpu.with_memory_space_constraint(value, pltpu.VMEM)


def layer(
    node_irreps,
    positions,
    send_list,
    neighbours,
    displacements,
    order_zero,
    order_one,
    order_two,
    reciprocal_triples,
    reciprocal_filter,
    cotangent,
):
    sizes = tuple(lax.axis_size(axis) for axis in AXES)
    irreps = jnp.transpose(node_irreps[0, 0, 0], (1, 0, 2))
    harmonics, atoms, width = irreps.shape
    sent = send_list[0, 0, 0]
    offered = sent.shape[0]
    neighbour = neighbours[0, 0, 0]
    waves = reciprocal_filter.shape[0]
    total_atoms = atoms * math.prod(sizes)
    own_cotangent = cotangent[0, 0, 0]

    tiles, own_atoms = pl.pallas_call(
        functools.partial(pack_kernel, sizes),
        out_shape=[
            jax.ShapeDtypeStruct((count, atoms, width), bf16)
            for count in (atom_tiles + slot_tiles, atom_tiles)
        ],
        in_specs=[far() for _ in range(4)],
        out_specs=[vmem() for _ in range(2)],
        scratch_shapes=[
            pltpu.SMEM(sent.shape, jnp.int32),
            pltpu.VMEM(irreps.shape, bf16),
            pltpu.VMEM((3, 1, atoms), f32),
            pltpu.VMEM(own_cotangent.shape, f32),
            pltpu.SemaphoreType.DMA((4,)),
        ],
        compiler_params=grant(4),
        name="pack",
    )(*map(stay, (sent, irreps, positions[0, 0, 0][:, None, :], own_cotangent)))

    atom_arrays, atom_spots, halo_arrays, halo_spots, shares = exchange(tiles, own_atoms, sizes)
    pieces = tuple(2 if size == 2 else 3 for size in sizes)
    depth = -(-(atoms + offered * math.prod(pieces)) // 256) * 256

    weights, spread, strengths = pl.pallas_call(
        functools.partial(prepare_kernel, pieces, offered),
        out_shape=(
            jax.ShapeDtypeStruct((2 * len(groups) * atoms, depth), bf16),
            jax.ShapeDtypeStruct((waves // shares, width), bf16),
            jax.ShapeDtypeStruct((waves // shares, width), f32),
        ),
        in_specs=[vmem(), vmem(), vmem(), far()],
        out_specs=(vmem(), vmem(), vmem()),
        scratch_shapes=[pltpu.SemaphoreType.DMA],
        compiler_params=grant(6),
        name="prepare",
    )(
        *map(near, (neighbour, displacements[0, 0, 0][:, None, :], reciprocal_triples.T)), stay(reciprocal_filter)
    )

    wave_step = math.gcd(256, waves // shares)
    steps = waves // shares // wave_step
    early, late = (atom_spots[: len(atom_spots) // 2], atom_spots[len(atom_spots) // 2 :]) if shares > 1 else (atom_spots, [])
    early_arrays = atom_arrays[: len(early)]
    late_arrays = atom_arrays[len(early) :]
    late = [(number - len(early), first, blocks) for number, first, blocks in late]

    def laid_out(spots):
        rows = atoms * sum(spot[2] for spot in spots)
        widths = (2 * width, width, width) if rows else ()
        return [pltpu.VMEM((rows, lanes), bf16) for lanes in widths]

    sums, plane, charge = pl.pallas_call(
        functools.partial(factor_kernel, tuple(early), wave_step, len(early_arrays)),
        out_shape=(
            jax.ShapeDtypeStruct((steps, 2 * wave_step, 2 * width), f32),
            jax.ShapeDtypeStruct((steps, 2 * wave_step, 1), f32),
            jax.ShapeDtypeStruct((1, width), f32),
        ),
        in_specs=[vmem() for _ in range(len(early_arrays) + 1)],
        out_specs=tuple(vmem() for _ in range(3)),
        scratch_shapes=laid_out(early),
        compiler_params=grant(6 + total_atoms // 256),
        name="factors",
    )(*map(near, (*early_arrays, spread)))
    part_shape = jax.ShapeDtypeStruct((3, atoms, width), f32)
    parts = pl.pallas_call(
        functools.partial(ewald_kernel, tuple(late), wave_step, total_atoms, shares, len(late_arrays)),
        out_shape=[part_shape] * shares,
        in_specs=[vmem() for _ in range(len(late_arrays) + 6)],
        out_specs=[vmem()] * shares,
        scratch_shapes=[pltpu.VMEM((2, steps, 2 * wave_step, 2 * width), bf16)] + laid_out(late),
        compiler_params=grant(6 + total_atoms // 256),
        name="ewald",
    )(*map(near, (*late_arrays, atom_arrays[0], spread, strengths, sums, plane, charge)))
    parts = list(parts)
    if shares > 1:
        parts[1] = swap(parts[1], sizes, lambda x, y, z: (x, y ^ 1, z))

    scale = 1.0 / math.sqrt(total_atoms * waves)
    updated, long_range, charge_grad, position_grad = pl.pallas_call(
        functools.partial(edge_kernel, sizes, scale, tuple(halo_spots), shares),
        out_shape=(
            jax.ShapeDtypeStruct((harmonics, atoms, width), bf16),
            jax.ShapeDtypeStruct((atoms, width), f32),
            jax.ShapeDtypeStruct((atoms, width), f32),
            jax.ShapeDtypeStruct((3, 1, atoms), f32),
        ),
        in_specs=[vmem() for _ in range(len(halo_arrays) + shares + 5)],
        out_specs=tuple(vmem() for _ in range(4)),
        scratch_shapes=[pltpu.VMEM((depth, len(slots) * width), bf16)],
        compiler_params=grant(6),
        name="edges",
    )(*map(near, (*halo_arrays, *parts, irreps, weights, order_zero, order_one, order_two)))
    outs = (jnp.transpose(updated, (1, 0, 2)), long_range, charge_grad, position_grad[:, 0, :])
    return tuple(out[None, None, None] for out in outs)


def solution(mesh):
    return jax.shard_map(
        layer,
        mesh=mesh,
        in_specs=(
            P("gx", "gy", "gz", None, None, None),
            P("gx", "gy", "gz", None, None),
            P("gx", "gy", "gz", None),
            P("gx", "gy", "gz", None, None),
            P("gx", "gy", "gz", None, None),
            P(),
            P(),
            P(),
            P(),
            P(),
            P("gx", "gy", "gz", None, None),
        ),
        out_specs=(
            P("gx", "gy", "gz", None, None, None),
            P("gx", "gy", "gz", None, None),
            P("gx", "gy", "gz", None, None),
            P("gx", "gy", "gz", None, None),
        ),
        check_vma=False,
    )
```
